32 devices in a mesh: dp: 16 (over z, y, x), tensor: 2 (over core).
Axes of the slice: x: 2, y: 2, z: 4, core: 2. Of those that a mesh axis runs over, the one named last changes fastest.
Arguments:
- tokens: bfloat16 [16384, 1536], P(('dp', 'tensor')), may hold values from -6 to 6
- segment_ids: int32 [16, 1024], P('dp'), may hold values from 0 to 7, never falling along the last dimension, each value on 1 to 512 neighbouring positions
- first_gain: float32 [1536], replicated, may hold values from 0.25 to 1.75
- query_weight: bfloat16 [1536, 1536], P(None, 'tensor'), may hold values from -0.15625 to 0.15625
- key_weight: bfloat16 [1536, 1536], P(None, 'tensor'), may hold values from -0.15625 to 0.15625
- value_weight: bfloat16 [1536, 1536], P(None, 'tensor'), may hold values from -0.15625 to 0.15625
- outgate_weight: bfloat16 [1536, 1536], P(None, 'tensor'), may hold values from -0.15625 to 0.15625
- forget_weight: bfloat16 [1536, 24], P(None, 'tensor'), may hold values from -0.15625 to 0.15625
- forget_bias: float32 [24], P('tensor'), may hold values from 1 to 12
- output_weight: bfloat16 [1536, 1536], P('tensor'), may hold values from -0.875 to 0.875
- second_gain: float32 [1536], replicated, may hold values from 0.25 to 1.75
- gate_weight: bfloat16 [1536, 4096], P(None, 'tensor'), may hold values from -0.15625 to 0.15625
- up_weight: bfloat16 [1536, 4096], P(None, 'tensor'), may hold values from -0.15625 to 0.15625
- down_weight: bfloat16 [4096, 1536], P('tensor'), may hold values from -0.09375 to 0.09375
- cotangent: bfloat16 [16384, 1536], P(('dp', 'tensor')), may hold values from -6 to 6
Outputs:
- result: bfloat16 [16384, 1536], P(('dp', 'tensor'))
- grad_tokens: float32 [16384, 1536], P(('dp', 'tensor'))
- grad_first: float32 [1536], replicated
- grad_query: float32 [1536, 1536], P('dp', 'tensor')
- grad_key: float32 [1536, 1536], P('dp', 'tensor')
- grad_value: float32 [1536, 1536], P('dp', 'tensor')
- grad_outgate: float32 [1536, 1536], P('dp', 'tensor')
- grad_forget: float32 [1536, 24], P('dp', 'tensor')
- grad_bias: float32 [24], replicated
- grad_output: float32 [1536, 1536], P('tensor', 'dp')
- grad_second: float32 [1536], replicated
- grad_gate: float32 [1536, 4096], P('dp', 'tensor')
- grad_up: float32 [1536, 4096], P('dp', 'tensor')
- grad_down: float32 [4096, 1536], P('tensor', 'dp')
The draws below stay inside these ranges and needn't reach their ends.
Inputs may be any that keep to these rules, and one draw needn't show every extreme that they name: `segment_ids`: ids never fall along a sequence; each document has 1 to 512 tokens and one of each sequence has exactly 512.
All inputs are finite; a program needn't handle non-finite values.
Results may differ from the reference program's by a relative error of at most 0.022.
Values may be sent and summed in bfloat16 or wider, within the bound.
A program may use at most 320 MiB of HBM per device.

```python
import math
import jax
import jax.numpy as jnp
import numpy as np
from jax import lax

D = 1536
HEADS = 24
HEAD_DIM = 64
FF = 4096
SEQ_LEN = 1024
SEQS_DEV = 1
DOCS = 8
MOST_DOC = 512
SEQS = 16
TOKENS = 16384
N_DP = 16


def draw_forget_bias(key, part):
    uniform_draw = jax.random.uniform(key, (HEADS,), jnp.float32)
    slow_rate = 0.3 / SEQ_LEN
    fast_rate = 1.0 / 25.0
    log_slow = jnp.log(jnp.float32(slow_rate))
    log_fast = jnp.log(jnp.float32(fast_rate))
    forget_rate = jnp.exp(log_slow + uniform_draw * (log_fast - log_slow))
    return jnp.log(1.0 / forget_rate - 1.0).astype(jnp.float32)


def with_spikes(drawn, rng, source, target, parts, factor):
    def block_of(position):
        return (jnp.arange(drawn.shape[position]) // (drawn.shape[position] // parts)).reshape((-1,) + (1,) * (drawn.ndim - 1 - position))

    one_side = jax.random.permutation(rng, parts)[block_of(target)]
    other_side = (block_of(target) + parts // 2) % parts
    return jnp.where((block_of(source) == one_side) | (block_of(source) == other_side), factor * drawn, drawn)


def shard_levels(stream_key, shape, cuts, smallest, top_value):
    def one(position, blocks):
        draws = jax.random.uniform(jax.random.fold_in(jax.random.fold_in(stream_key, 6), position), (blocks,), jnp.float32, smallest / len(cuts), top_value / len(cuts))
        return jnp.repeat(jnp.exp(draws), shape[position] // blocks).reshape((-1,) + (1,) * (len(shape) - position - 1))

    level = one(*cuts[0])
    for cut in cuts[1:]:
        level = level * one(*cut)
    return level


def profile(number_of, total, limit, skew):
    weights = [(1 << 20) // math.isqrt(grade ** skew) + 1 for grade in range(2, number_of + 1)]
    surplus, holding = total - limit - (number_of - 1), [1] * (number_of - 1)
    while surplus > 0:
        free = [i for i in range(number_of - 1) if holding[i] < limit]
        mass, left = sum([weights[i] for i in free]), surplus
        for i in free:
            addition = min(limit - holding[i], max(1, left * weights[i] // mass), surplus)
            holding[i] = holding[i] + addition
            surplus = surplus - addition
    return np.array([limit] + holding)


def ragged(stream_key, number_of, total, reach, skew):
    if number_of == 2:
        one = jax.random.randint(stream_key, (), max(1, total - reach), min(reach, total - 1) + 1)
        return jnp.stack([one, total - one])
    tallies = jnp.asarray(profile(number_of, total, reach, skew), jnp.int32)
    pairs = (number_of - 1) // 2
    giver, sink = tallies[1:1 + 2 * pairs:2], tallies[2:2 + 2 * pairs:2]
    margin = jnp.minimum(giver - 1, reach - sink)
    shifted = jax.random.randint(jax.random.fold_in(stream_key, 1), (pairs,), 0, 1 << 20) % (margin + 1)
    tallies = tallies.at[1:1 + 2 * pairs:2].set(giver - shifted).at[2:2 + 2 * pairs:2].set(sink + shifted)
    return tallies[jax.random.permutation(jax.random.fold_in(stream_key, 2), number_of)]


def noise(stream_key, extent, spread, bound, split=(), kind=jnp.bfloat16):
    factor_of = shard_levels(stream_key, extent, split, -0.22, 0.18) if split else 1.0
    entries = jax.random.normal(stream_key, extent, jnp.float32) * spread * factor_of
    return jnp.minimum(jnp.maximum(entries, -bound), bound).astype(kind)


def heavy_noise(stream_key, extent, width, most, shards, heavy, held_as=jnp.bfloat16):
    array = width * jax.random.normal(stream_key, extent, jnp.float32)
    if shards:
        array = array * shard_levels(stream_key, extent, shards, -0.22, 0.18)
    return jnp.clip(with_spikes(array, jax.random.fold_in(stream_key, 3), *heavy), -most, most).astype(held_as)


def setup_inputs(seed: int = 0) -> dict:
    keys = jax.random.split(jax.random.key(seed), 16)
    tokens = noise(keys[0], (TOKENS, D), 1.0, 6.0, ((0, 32),))
    segment_ids = jax.vmap(lambda own: jnp.searchsorted(jnp.cumsum(ragged(own, DOCS, SEQ_LEN, MOST_DOC, 2)), jnp.arange(SEQ_LEN), side="right"))(jax.random.split(keys[1], SEQS)).reshape((SEQS, SEQ_LEN)).astype(jnp.int32)
    first_gain = jnp.clip(1.0 + 0.15 * jax.random.normal(keys[2], (D,), jnp.float32), 0.25, 1.75)
    query_weight = noise(keys[3], (D, D), D ** -0.5, 0.15625, ((1, 2),))
    key_weight = noise(keys[4], (D, D), D ** -0.5, 0.15625, ((1, 2),))
    value_weight = noise(keys[5], (D, D), D ** -0.5, 0.15625, ((1, 2),))
    outgate_weight = noise(keys[6], (D, D), D ** -0.5, 0.15625, ((1, 2),))
    forget_weight = noise(keys[7], (D, HEADS), D ** -0.5, 0.15625, ((1, 2),))
    forget_bias = draw_forget_bias(jax.random.fold_in(keys[15], 71), 0)
    output_weight = noise(keys[9], (D, D), (D // 32) ** -0.5, 0.875, ((0, 2),))
    second_gain = jnp.clip(1.0 + 0.15 * jax.random.normal(keys[10], (D,), jnp.float32), 0.25, 1.75)
    gate_weight = noise(keys[11], (D, FF), D ** -0.5, 0.15625, ((1, 2),))
    up_weight = noise(keys[12], (D, FF), D ** -0.5, 0.15625, ((1, 2),))
    down_weight = noise(keys[13], (FF, D), FF ** -0.5, 0.09375, ((0, 2),))
    cotangent = heavy_noise(keys[14], (TOKENS, D), 1.0, 6.0, ((0, 32),), (0, 1, 32, 2.75))
    return {"tokens": tokens, "segment_ids": segment_ids, "first_gain": first_gain, "query_weight": query_weight, "key_weight": key_weight, "value_weight": value_weight, "outgate_weight": outgate_weight, "forget_weight": forget_weight, "forget_bias": forget_bias, "output_weight": output_weight, "second_gain": second_gain, "gate_weight": gate_weight, "up_weight": up_weight, "down_weight": down_weight, "cotangent": cotangent}


epsilon = 1e-06
masked_value = -1e+30
highest = lax.Precision.HIGHEST

@jax.custom_vjp
def low(v):
    return lax.optimization_barrier(v.astype(jnp.bfloat16)).astype(jnp.float32)

@jax.custom_vjp
def low_back(v):
    return v

def low_keep(v):
    return (low(v), None)

def low_pass(kept, grad):
    return (grad,)

def back_keep(v):
    return (v, None)

def back_low(kept, grad):
    return (low(grad),)
low.defvjp(low_keep, low_pass)
low_back.defvjp(back_keep, back_low)

def product(former, latter):
    return jnp.dot(former, latter, precision=highest)

def norm_rows(matrix, gain_vec):
    return matrix * lax.rsqrt(lax.optimization_barrier(jnp.mean(matrix * matrix, axis=1, keepdims=True)) + epsilon) * gain_vec

def attend(pieces):
    query_rows, key_rows, value_rows, decays, segment = pieces
    query_heads = query_rows.reshape(SEQ_LEN, HEADS, HEAD_DIM)
    key_heads = key_rows.reshape(SEQ_LEN, HEADS, HEAD_DIM)
    value_heads = value_rows.reshape(SEQ_LEN, HEADS, HEAD_DIM)
    scores = jnp.einsum('qhd,khd->hqk', query_heads, key_heads, precision=highest) * HEAD_DIM ** (-0.5)
    decay_t = decays.T
    scores = low_back(scores + decay_t[:, :, None] - decay_t[:, None, :])
    places = jnp.arange(SEQ_LEN, dtype=jnp.int32)
    allowed = (places[None, :] <= places[:, None]) & (segment[:, None] == segment[None, :])
    scores = jnp.where(allowed[None], scores, masked_value)
    row_peak = lax.optimization_barrier(jnp.max(scores, axis=2, keepdims=True))
    exp_scores = jnp.exp(scores - row_peak)
    weights = exp_scores / lax.optimization_barrier(jnp.sum(exp_scores, axis=2, keepdims=True))
    mixed_out = jnp.einsum('hqk,khd->qhd', low(weights), value_heads, precision=highest)
    return low_back(mixed_out.reshape(SEQ_LEN, HEADS * HEAD_DIM))

def by_sequence(stacked):
    return stacked.reshape(SEQS_DEV, SEQ_LEN, stacked.shape[1])

def layer(inputs, segments, first_gain, query_weight, key_weight, value_weight, outgate_weight, forget_weight, forget_bias, output_weight, second_gain, gate_weight, up_weight, down_weight):
    first_rows = low(norm_rows(inputs, first_gain))
    query_rows = low(low_back(product(first_rows, query_weight)))
    key_rows = low(low_back(product(first_rows, key_weight)))
    value_rows = low(low_back(product(first_rows, value_weight)))
    outgate = jax.nn.sigmoid(low_back(product(first_rows, outgate_weight)))
    forget_logit = low_back(product(first_rows, forget_weight) + forget_bias)
    decays = jnp.cumsum(jax.nn.log_sigmoid(forget_logit).reshape(SEQS_DEV, SEQ_LEN, HEADS), axis=1)
    mixed_out = lax.map(jax.checkpoint(attend), (by_sequence(query_rows), by_sequence(key_rows), by_sequence(value_rows), decays, segments))
    mixed_out = mixed_out.reshape(SEQS_DEV * SEQ_LEN, D)
    gated_out = low(mixed_out * outgate)
    middle = inputs + low_back(product(gated_out, output_weight))
    second_rows = low(norm_rows(middle, second_gain))
    gate_pre = low_back(product(second_rows, gate_weight))
    up_pre = low_back(product(second_rows, up_weight))
    hidden = low(jax.nn.silu(gate_pre) * up_pre)
    return middle + product(hidden, down_weight)

def reference(tokens, segment_ids, first_gain, query_weight, key_weight, value_weight, outgate_weight, forget_weight, forget_bias, output_weight, second_gain, gate_weight, up_weight, down_weight, cotangent):
    params = tuple((item.astype(jnp.float32) for item in (first_gain, query_weight, key_weight, value_weight, outgate_weight, forget_weight, forget_bias, output_weight, second_gain, gate_weight, up_weight, down_weight)))
    group_rows = SEQS_DEV * SEQ_LEN
    inputs = tokens.astype(jnp.float32).reshape(N_DP, group_rows, D)
    upstream = cotangent.astype(jnp.float32).reshape(N_DP, group_rows, D)
    segments = segment_ids.reshape(N_DP, SEQS_DEV, SEQ_LEN)

    def group(running, pieces):
        group_in, segment_rows, upstream_rows = pieces

        def forward(rows_in, *weights_in):
            return layer(rows_in, segment_rows, *weights_in)
        outputs, pullback = jax.vjp(forward, group_in, *params)
        grad_list = pullback(upstream_rows)
        new_running = tuple((before + added for before, added in zip(running, grad_list[1:])))
        return (new_running, (outputs.astype(jnp.bfloat16), grad_list[0]))
    zero_sums = tuple((jnp.zeros(item.shape, jnp.float32) for item in params))
    sums, (result, input_grad) = lax.scan(group, zero_sums, (inputs, segments, upstream))
    return (result.reshape(TOKENS, D), input_grad.reshape(TOKENS, D), sums[0], sums[1], sums[2], sums[3], sums[4], sums[5], sums[6], sums[7], sums[8], sums[9], sums[10], sums[11])
```

```python
from functools import partial

import jax
import jax.numpy as jnp
from jax import lax
from jax.sharding import PartitionSpec as P

epsilon = 1e-06
masked_value = -1e30


def matmul(former, latter):
    return jnp.dot(former, latter, preferred_element_type=jnp.float32)


def inner_rows(former, latter):
    return lax.dot_general(
        former, latter, (((0,), (0,)), ((), ())), preferred_element_type=jnp.float32
    )


def against(former, latter):
    return lax.dot_general(
        former, latter, (((1,), (1,)), ((), ())), preferred_element_type=jnp.float32
    )


def norm_scale(matrix):
    return lax.rsqrt(jnp.mean(matrix * matrix, axis=1, keepdims=True) + epsilon)


def norm_back(upstream, normed, scaling, gain_vec):
    weighted = upstream * gain_vec
    return scaling * (weighted - normed * jnp.mean(weighted * normed, axis=1, keepdims=True))


def halve(stacked, bit, axis, wide):
    mine = (lax.axis_index("dp") >> bit) & 1
    count = lax.axis_size("dp")
    sent = lax.ppermute(
        lax.dynamic_index_in_dim(stacked, 1 - mine, axis, keepdims=False),
        "dp",
        [(place, place ^ (1 << bit)) for place in range(count)],
    )
    kept = lax.dynamic_index_in_dim(stacked, mine, axis, keepdims=False)
    total = kept.astype(jnp.float32) + sent.astype(jnp.float32)
    return total if wide else total.astype(jnp.bfloat16)


def spread_sum(gradient, swap):
    count = lax.axis_size("dp")
    bits = count.bit_length() - 1
    order = list(range(bits))
    for front, back in swap:
        order[front], order[back] = order[back], order[front]
    live = list(range(bits - 1, -1, -1))
    stacked = gradient.reshape((2,) * bits + (gradient.shape[0] // count, gradient.shape[1]))
    for place, bit in enumerate(order):
        axis = live.index(bit)
        live.pop(axis)
        stacked = halve(stacked, bit, axis, place == bits - 1)
    return stacked


def raw_scores(query_rows, key_rows, decays, segment, head_dim):
    length = query_rows.shape[0]
    head_count = decays.shape[1]
    query_heads = query_rows.reshape(length, head_count, head_dim)
    key_heads = key_rows.reshape(length, head_count, head_dim)
    scores = jnp.einsum("qhd,khd->hqk", query_heads, key_heads, preferred_element_type=jnp.float32)
    scores = scores * float(head_dim) ** (-0.5)
    decay_t = decays.T
    scores = scores + decay_t[:, :, None] - decay_t[:, None, :]
    places = lax.iota(jnp.int32, length)
    allowed = (places[None, :] <= places[:, None]) & (segment[:, None] == segment[None, :])
    return (jnp.where(allowed[None], scores, masked_value), query_heads, key_heads)


def attend_forward(pieces, head_dim):
    query_rows, key_rows, value_rows, decays, segment = pieces
    length = query_rows.shape[0]
    head_count = decays.shape[1]
    scores, query_heads, key_heads = raw_scores(query_rows, key_rows, decays, segment, head_dim)
    row_peak = jnp.max(scores, axis=2, keepdims=True)
    exp_scores = jnp.exp(scores - row_peak)
    row_total = jnp.sum(exp_scores, axis=2, keepdims=True)
    probs_low = (exp_scores / row_total).astype(jnp.bfloat16)
    value_heads = value_rows.reshape(length, head_count, head_dim)
    mixed_out = jnp.einsum(
        "hqk,khd->qhd", probs_low, value_heads, preferred_element_type=jnp.float32
    )
    logsum = row_peak[:, :, 0] + jnp.log(row_total[:, :, 0])
    return (mixed_out.reshape(length, head_count * head_dim), logsum)


def attend_backward(pieces, head_dim):
    query_rows, key_rows, value_rows, decays, segment, logsum, mixed_grad = pieces
    length = query_rows.shape[0]
    head_count = decays.shape[1]
    scaling = float(head_dim) ** (-0.5)
    scores, query_heads, key_heads = raw_scores(query_rows, key_rows, decays, segment, head_dim)
    probs = jnp.exp(scores - logsum[:, :, None])
    probs_low = probs.astype(jnp.bfloat16)
    value_heads = value_rows.reshape(length, head_count, head_dim)
    grad_heads = mixed_grad.reshape(length, head_count, head_dim)
    value_grad = jnp.einsum(
        "hqk,qhd->khd", probs_low, grad_heads, preferred_element_type=jnp.float32
    )
    prob_grad = jnp.einsum(
        "qhd,khd->hqk", grad_heads, value_heads, preferred_element_type=jnp.float32
    )
    row_delta = jnp.sum(probs * prob_grad, axis=2, keepdims=True)
    score_grad = (probs * (prob_grad - row_delta)).astype(jnp.bfloat16)
    query_grad = (
        jnp.einsum("hqk,khd->qhd", score_grad, key_heads, preferred_element_type=jnp.float32)
        * scaling
    )
    key_grad = (
        jnp.einsum("hqk,qhd->khd", score_grad, query_heads, preferred_element_type=jnp.float32)
        * scaling
    )
    grad_wide = score_grad.astype(jnp.float32)
    decay_grad = (jnp.sum(grad_wide, axis=2) - jnp.sum(grad_wide, axis=1)).T
    full_width = head_count * head_dim
    return (
        query_grad.reshape(length, full_width).astype(jnp.bfloat16),
        key_grad.reshape(length, full_width).astype(jnp.bfloat16),
        value_grad.reshape(length, full_width).astype(jnp.bfloat16),
        decay_grad,
    )


def local(
    tokens,
    segment_ids,
    first_gain,
    query_weight,
    key_weight,
    value_weight,
    outgate_weight,
    forget_weight,
    forget_bias,
    output_weight,
    second_gain,
    gate_weight,
    up_weight,
    down_weight,
    cotangent,
):
    local_heads = forget_weight.shape[1]
    head_dim = query_weight.shape[1] // local_heads
    sequences = segment_ids.shape[0]
    length = segment_ids.shape[1]

    def by_sequence(stacked):
        return stacked.reshape(sequences, length, stacked.shape[1])

    inputs = tokens.astype(jnp.float32)
    scale_one = norm_scale(inputs)
    normed_one = inputs * scale_one
    first_rows = (normed_one * first_gain).astype(jnp.bfloat16)
    first_all = lax.all_gather(first_rows, "tensor", axis=0, tiled=True)
    query_rows = matmul(first_all, query_weight).astype(jnp.bfloat16)
    key_rows = matmul(first_all, key_weight).astype(jnp.bfloat16)
    value_rows = matmul(first_all, value_weight).astype(jnp.bfloat16)
    outgate = jax.nn.sigmoid(matmul(first_all, outgate_weight))
    forget_logit = matmul(first_all, forget_weight) + forget_bias
    decays = jnp.cumsum(
        jax.nn.log_sigmoid(forget_logit).reshape(sequences, length, local_heads), axis=1
    )
    mixed_seq, logsum = lax.map(
        partial(attend_forward, head_dim=head_dim),
        (
            by_sequence(query_rows),
            by_sequence(key_rows),
            by_sequence(value_rows),
            decays,
            segment_ids,
        ),
    )
    head_width = query_rows.shape[1]
    mixed_out = mixed_seq.reshape(sequences * length, head_width)
    gated_out = (mixed_out * outgate).astype(jnp.bfloat16)
    attn_rows = lax.psum_scatter(
        matmul(gated_out, output_weight), "tensor", scatter_dimension=0, tiled=True
    )
    middle = inputs + attn_rows
    scale_two = norm_scale(middle)
    normed_two = middle * scale_two
    second_rows = (normed_two * second_gain).astype(jnp.bfloat16)
    second_all = lax.all_gather(second_rows, "tensor", axis=0, tiled=True)
    gate_pre = matmul(second_all, gate_weight)
    up_pre = matmul(second_all, up_weight)
    sigmoid_gate = jax.nn.sigmoid(gate_pre)
    swish_out = gate_pre * sigmoid_gate
    hidden = (swish_out * up_pre).astype(jnp.bfloat16)
    mlp_rows = lax.psum_scatter(
        matmul(hidden, down_weight).astype(jnp.bfloat16), "tensor", scatter_dimension=0, tiled=True
    ).astype(jnp.float32)
    result = (middle + mlp_rows).astype(jnp.bfloat16)
    upstream = lax.all_gather(cotangent, "tensor", axis=0, tiled=True)
    hidden_grad = against(upstream, down_weight)
    gate_grad = (
        hidden_grad * up_pre * sigmoid_gate * (1.0 + gate_pre * (1.0 - sigmoid_gate))
    ).astype(jnp.bfloat16)
    up_grad = (hidden_grad * swish_out).astype(jnp.bfloat16)
    grad_gate = inner_rows(second_all, gate_grad)
    grad_up = inner_rows(second_all, up_grad)
    second_grad = lax.psum_scatter(
        against(gate_grad, gate_weight) + against(up_grad, up_weight),
        "tensor",
        scatter_dimension=0,
        tiled=True,
    )
    middle_grad = cotangent.astype(jnp.float32) + norm_back(
        second_grad, normed_two, scale_two, second_gain
    )
    gain_two_part = jnp.sum(second_grad * normed_two, axis=0)
    middle_low = middle_grad.astype(jnp.bfloat16)
    middle_all = lax.all_gather(middle_low, "tensor", axis=0, tiled=True)
    grad_output = inner_rows(middle_all, gated_out)
    gated_grad = against(middle_all, output_weight)
    mixed_grad = (gated_grad * outgate).astype(jnp.bfloat16)
    outgate_grad = (gated_grad * mixed_out * outgate * (1.0 - outgate)).astype(jnp.bfloat16)
    grad_outgate = inner_rows(first_all, outgate_grad)
    query_seq, key_seq, value_seq, decay_grad = lax.map(
        partial(attend_backward, head_dim=head_dim),
        (
            by_sequence(query_rows),
            by_sequence(key_rows),
            by_sequence(value_rows),
            decays,
            segment_ids,
            logsum,
            by_sequence(mixed_grad),
        ),
    )
    query_grad = query_seq.reshape(sequences * length, head_width)
    key_grad = key_seq.reshape(sequences * length, head_width)
    value_grad = value_seq.reshape(sequences * length, head_width)
    log_grad = jnp.flip(jnp.cumsum(jnp.flip(decay_grad, 1), axis=1), 1).reshape(
        sequences * length, local_heads
    )
    forget_grad = (log_grad * jax.nn.sigmoid(-forget_logit)).astype(jnp.bfloat16)
    grad_query = inner_rows(first_all, query_grad)
    grad_key = inner_rows(first_all, key_grad)
    grad_value = inner_rows(first_all, value_grad)
    grad_forget = inner_rows(first_all, forget_grad)
    bias_part = jnp.sum(forget_grad.astype(jnp.float32), axis=0)
    total = against(query_grad, query_weight)
    total = total + against(key_grad, key_weight)
    total = total + against(value_grad, value_weight)
    total = total + against(outgate_grad, outgate_weight)
    first_grad = lax.psum_scatter(
        (total + against(forget_grad, forget_weight)).astype(jnp.bfloat16),
        "tensor",
        scatter_dimension=0,
        tiled=True,
    ).astype(jnp.float32)
    tokens_grad = middle_grad + norm_back(first_grad, normed_one, scale_one, first_gain)
    gain_one_part = jnp.sum(first_grad * normed_one, axis=0)
    placed = lax.dynamic_update_slice(
        jnp.zeros((local_heads * lax.axis_size("tensor"),), jnp.float32),
        bias_part,
        (lax.axis_index("tensor") * local_heads,),
    )
    gain_one, gain_two, bias_total = lax.psum(
        (gain_one_part, gain_two_part, placed), ("dp", "tensor")
    )
    along, across, deep = (), ((0, 1),), ((0, 2),)
    low = jnp.bfloat16
    half = hidden.shape[1] // 2
    down_grads = [
        spread_sum(inner_rows(upstream, hidden[:, :half]).astype(low), along),
        spread_sum(inner_rows(upstream, hidden[:, half:]).astype(low), across),
    ]
    summed = (
        spread_sum(grad_query.astype(low), along),
        spread_sum(grad_key.astype(low), across),
        spread_sum(grad_value.astype(low), deep),
        spread_sum(grad_outgate.astype(low), across),
        spread_sum(grad_forget.astype(low), along),
        spread_sum(grad_output.astype(low), along).T,
        spread_sum(grad_gate.astype(low), along),
        spread_sum(grad_up.astype(low), across),
        jnp.concatenate(down_grads, axis=1).T,
    )
    return (
        result,
        tokens_grad,
        gain_one,
        summed[0],
        summed[1],
        summed[2],
        summed[3],
        summed[4],
        bias_total,
        summed[5],
        gain_two,
        summed[6],
        summed[7],
        summed[8],
    )


def solution(mesh):
    in_specs = (
        P(("dp", "tensor"), None),
        P("dp", None),
        P(),
        P(None, "tensor"),
        P(None, "tensor"),
        P(None, "tensor"),
        P(None, "tensor"),
        P(None, "tensor"),
        P("tensor"),
        P("tensor", None),
        P(),
        P(None, "tensor"),
        P(None, "tensor"),
        P("tensor", None),
        P(("dp", "tensor"), None),
    )
    out_specs = (
        P(("dp", "tensor"), None),
        P(("dp", "tensor"), None),
        P(),
        P("dp", "tensor"),
        P("dp", "tensor"),
        P("dp", "tensor"),
        P("dp", "tensor"),
        P("dp", "tensor"),
        P(),
        P("tensor", "dp"),
        P(),
        P("dp", "tensor"),
        P("dp", "tensor"),
        P("tensor", "dp"),
    )
    return jax.shard_map(local, mesh=mesh, in_specs=in_specs, out_specs=out_specs, check_vma=False)
```

```python
from functools import partial

import jax
import jax.numpy as jnp
from jax import lax
from jax.experimental import pallas as pl
from jax.experimental.pallas import tpu as pltpu
from jax.sharding import PartitionSpec as P

epsilon = 1e-06
masked_value = -1e30


def matmul(former, latter):
    return jnp.dot(former, latter, preferred_element_type=jnp.float32)


def inner_rows(former, latter):
    return lax.dot_general(
        former, latter, (((0,), (0,)), ((), ())), preferred_element_type=jnp.float32
    )


def against(former, latter):
    return lax.dot_general(
        former, latter, (((1,), (1,)), ((), ())), preferred_element_type=jnp.float32
    )


def norm_scale(matrix):
    return lax.rsqrt(jnp.mean(matrix * matrix, axis=1, keepdims=True) + epsilon)


def norm_back(upstream, normed, scaling, gain_vec):
    weighted = upstream * gain_vec
    return scaling * (weighted - normed * jnp.mean(weighted * normed, axis=1, keepdims=True))


def halve(stacked, bit, axis, wide):
    mine = (lax.axis_index("dp") >> bit) & 1
    count = lax.axis_size("dp")
    sent = lax.ppermute(
        lax.dynamic_index_in_dim(stacked, 1 - mine, axis, keepdims=False),
        "dp",
        [(place, place ^ (1 << bit)) for place in range(count)],
    )
    kept = lax.dynamic_index_in_dim(stacked, mine, axis, keepdims=False)
    total = kept.astype(jnp.float32) + sent.astype(jnp.float32)
    return total if wide else total.astype(jnp.bfloat16)


def spread_sum(gradient, swap):
    count = lax.axis_size("dp")
    bits = count.bit_length() - 1
    order = list(range(bits))
    for front, back in swap:
        order[front], order[back] = order[back], order[front]
    live = list(range(bits - 1, -1, -1))
    stacked = gradient.reshape((2,) * bits + (gradient.shape[0] // count, gradient.shape[1]))
    for place, bit in enumerate(order):
        axis = live.index(bit)
        live.pop(axis)
        stacked = halve(stacked, bit, axis, place == bits - 1)
    return stacked


block_rows = 256
longest_doc = 512
low = jnp.bfloat16
log2e = 1.4426950408889634


def windows(length):
    reach = -(-(longest_doc - 1) // block_rows)
    spans = []
    place = 0
    for one in range(length // block_rows):
        start = max(0, one - reach) * block_rows
        width = (one + 1) * block_rows - start
        spans.append((one * block_rows, start, width, place))
        place += width
    return spans, place


def lane_of(shape):
    return lax.broadcasted_iota(jnp.int32, shape, len(shape) - 1)


def running(rows, back):
    length = rows.shape[1]
    lanes = lane_of(rows.shape)
    step = 1
    while step < length:
        if back:
            moved = jnp.where(lanes < length - step, pltpu.roll(rows, length - step, 1), 0.0)
        else:
            moved = jnp.where(lanes >= step, pltpu.roll(rows, step, 1), 0.0)
        rows = rows + moved
        step *= 2
    return rows


def log_sigmoid(value):
    return jnp.minimum(value, 0.0) - jnp.log1p(jnp.exp(-jnp.abs(value)))


def fill_bias(seg_col, seg_row, bias, spans):
    for first, start, width, place in spans:
        rows = first + lax.broadcasted_iota(jnp.int32, (block_rows, width), 0)
        cols = start + lax.broadcasted_iota(jnp.int32, (block_rows, width), 1)
        same = seg_col[first : first + block_rows, :] == seg_row[:, start : start + width]
        bias[:, place : place + width] = jnp.where((cols <= rows) & same, 0.0, masked_value)


def head_parts(block, head_dim, head, mark):
    lanes = lane_of(block.shape)
    kept = jnp.where(lanes // head_dim == head, block, jnp.zeros_like(block))
    if mark is None:
        return kept
    return jnp.where(lanes == mark, jnp.ones_like(block), kept)


def forward_body(q_ref, k_ref, v_ref, gate_ref, logit_ref, col_ref, row_ref, mixed_ref, gated_ref, peak_ref, bias, fall, *, head_dim, spans, heads):
    pair = pl.program_id(0)

    @pl.when(pair == 0)
    def _():
        fill_bias(col_ref[...], row_ref[...], bias, spans)
        fall[...] = running(log_sigmoid(logit_ref[...]), False) * log2e

    lanes = lane_of((block_rows, q_ref.shape[1]))
    falls = [fall[pl.ds(pair * heads + head, 1), :] for head in range(heads)]
    for first, start, width, place in spans:
        query = q_ref[first : first + block_rows, :]
        key = k_ref[start : start + width, :]
        value = v_ref[start : start + width, :]
        mixed = None
        peaks = None
        for head in range(heads):
            line = falls[head]
            shift = line[:, first : first + 1] - line[:, start : start + width]
            scores = lax.dot_general(
                head_parts(query, head_dim, head, None), key, (((1,), (1,)), ((), ())),
                preferred_element_type=jnp.float32,
            )
            scores = scores * (head_dim**-0.5 * log2e) + shift + bias[:, place : place + width]
            top = jnp.max(scores, axis=1, keepdims=True)
            weight = jnp.exp2(scores - top)
            total = jnp.sum(weight, axis=1, keepdims=True)
            weight = (weight * (1.0 / total)).astype(low)
            part = jnp.dot(weight, head_parts(value, head_dim, head, None), preferred_element_type=jnp.float32)
            peak = jnp.broadcast_to(top + jnp.log2(total), lanes.shape)
            mixed = part if mixed is None else mixed + part
            peaks = peak if peaks is None else jnp.where(lanes // head_dim == head, peak, peaks)
        rows = slice(first, first + block_rows)
        mixed_ref[rows, :] = mixed
        peak_ref[rows, :] = peaks
        gated_ref[rows, :] = (mixed * gate_ref[rows, :]).astype(low)


def attention_sizes(width, head_dim):
    wide = 128 if width % 128 == 0 and 128 % head_dim == 0 else width
    return wide, wide // head_dim


def attend_forward(query, key, value, outgate, logit_t, segment, head_dim):
    length, width = query.shape
    wide, heads = attention_sizes(width, head_dim)
    spans, total = windows(length)
    whole = pl.BlockSpec(memory_space=pltpu.VMEM)
    part = pl.BlockSpec((length, wide), lambda i: (0, i))
    rows = -(-logit_t.shape[0] // 8) * 8
    area = sum(span[2] for span in spans) * block_rows
    return pl.pallas_call(
        partial(forward_body, head_dim=head_dim, spans=spans, heads=heads),
        grid=(width // wide,),
        in_specs=[part, part, part, part, whole, whole, whole],
        out_specs=[part, part, part],
        out_shape=[
            jax.ShapeDtypeStruct((length, width), jnp.float32),
            jax.ShapeDtypeStruct((length, width), low),
            jax.ShapeDtypeStruct((length, width), jnp.float32),
        ],
        scratch_shapes=[
            pltpu.VMEM((block_rows, total), jnp.float32),
            pltpu.VMEM((rows, length), jnp.float32),
        ],
        compiler_params=pltpu.CompilerParams(vmem_limit_bytes=50 * 2**20),
        cost_estimate=pl.CostEstimate(
            flops=16 * area * width, bytes_accessed=20 * length * width, transcendentals=area * width // head_dim
        ),
        name="attend_forward",
    )(query, key, value, outgate, jnp.pad(logit_t, ((0, rows - logit_t.shape[0]), (0, 0))), segment.reshape(length, 1), segment.reshape(1, length))


def backward_body(q_ref, k_ref, v_ref, grad_ref, peak_ref, logit_ref, col_ref, row_ref, dq_ref, dk_ref, dv_ref, forget_ref, bias, fall, key_sum, value_sum, slope, *, head_dim, spans, heads):
    pair = pl.program_id(0)
    wide = q_ref.shape[1]

    @pl.when(pair == 0)
    def _():
        fill_bias(col_ref[...], row_ref[...], bias, spans)
        fall[...] = running(log_sigmoid(logit_ref[...]), False) * log2e
        slope[...] = jnp.zeros_like(slope)

    falls = [fall[pl.ds(pair * heads + head, 1), :] for head in range(heads)]
    scaling = head_dim**-0.5
    value_sum[...] = jnp.zeros_like(value_sum)
    key_sum[...] = jnp.zeros_like(key_sum)
    lanes = lane_of((block_rows, wide))
    slots = lane_of((block_rows, slope.shape[1]))
    marks = [((head + 1) * head_dim) % wide for head in range(heads)]
    for first, start, width, place in spans:
        rows = slice(first, first + block_rows)
        query = q_ref[rows, :]
        key = k_ref[start : start + width, :]
        value = v_ref[start : start + width, :]
        grad = grad_ref[rows, :]
        query_grad = None
        for head in range(heads):
            line = falls[head]
            shift = line[:, first : first + 1] - line[:, start : start + width]
            scores = lax.dot_general(
                head_parts(query, head_dim, head, None), key, (((1,), (1,)), ((), ())),
                preferred_element_type=jnp.float32,
            )
            peak = peak_ref[rows, head * head_dim : head * head_dim + 1]
            scores = scores * (scaling * log2e) + shift + bias[:, place : place + width]
            weight = jnp.exp2(scores - peak)
            own_grad = head_parts(grad, head_dim, head, None)
            rise = lax.dot_general(
                own_grad, value, (((1,), (1,)), ((), ())), preferred_element_type=jnp.float32
            )
            delta = jnp.sum(weight * rise, axis=1, keepdims=True)
            change = (weight * (rise - delta)).astype(low)
            weight = weight.astype(low)
            value_sum[start : start + width, :] += lax.dot_general(
                weight, own_grad, (((0,), (0,)), ((), ())), preferred_element_type=jnp.float32
            )
            mark = marks[head]
            from_key = jnp.dot(change, head_parts(key, head_dim, head, mark), preferred_element_type=jnp.float32)
            key_sum[head, start : start + width, :] += lax.dot_general(
                change, head_parts(query, head_dim, head, mark), (((0,), (0,)), ((), ())),
                preferred_element_type=jnp.float32,
            )
            slope[rows, :] += jnp.where(slots == pair * heads + head, from_key[:, mark : mark + 1], 0.0)
            query_grad = from_key if query_grad is None else jnp.where(lanes // head_dim == head, from_key, query_grad)
        dq_ref[rows, :] = (query_grad * scaling).astype(low)
    length = q_ref.shape[0]
    lanes = lane_of((length, wide))
    slots = lane_of(slope.shape)
    total = key_sum[0]
    gone = jnp.where(slots == pair * heads, total[:, marks[0] : marks[0] + 1], 0.0)
    for head in range(1, heads):
        other = key_sum[head]
        gone += jnp.where(slots == pair * heads + head, other[:, marks[head] : marks[head] + 1], 0.0)
        total = jnp.where(lanes // head_dim == head, other, total)
    slope[...] -= gone
    dk_ref[...] = (total * scaling).astype(low)
    dv_ref[...] = value_sum[...].astype(low)

    @pl.when(pair == pl.num_programs(0) - 1)
    def _():
        count = logit_ref.shape[0]
        turned = slope[...].T[:count, :]
        forget_ref[...] = (running(turned, True) * jax.nn.sigmoid(-logit_ref[...])).astype(low)


def attend_backward(query, key, value, mixed_grad, peaks, logit_t, segment, head_dim):
    length, width = query.shape
    wide, heads = attention_sizes(width, head_dim)
    spans, total = windows(length)
    whole = pl.BlockSpec(memory_space=pltpu.VMEM)
    part = pl.BlockSpec((length, wide), lambda i: (0, i))
    rows = -(-logit_t.shape[0] // 8) * 8
    area = sum(span[2] for span in spans) * block_rows
    return pl.pallas_call(
        partial(backward_body, head_dim=head_dim, spans=spans, heads=heads),
        grid=(width // wide,),
        in_specs=[part, part, part, part, part, whole, whole, whole],
        out_specs=[part, part, part, pl.BlockSpec((rows, length), lambda i: (0, 0))],
        out_shape=[jax.ShapeDtypeStruct((length, width), low)] * 3
        + [jax.ShapeDtypeStruct((rows, length), low)],
        scratch_shapes=[
            pltpu.VMEM((block_rows, total), jnp.float32),
            pltpu.VMEM((rows, length), jnp.float32),
            pltpu.VMEM((heads, length, wide), jnp.float32),
            pltpu.VMEM((length, wide), jnp.float32),
            pltpu.VMEM((length, 128), jnp.float32),
        ],
        compiler_params=pltpu.CompilerParams(vmem_limit_bytes=50 * 2**20),
        cost_estimate=pl.CostEstimate(
            flops=40 * area * width, bytes_accessed=20 * length * width, transcendentals=area * width // head_dim
        ),
        name="attend_backward",
    )(query, key, value, mixed_grad, peaks, jnp.pad(logit_t, ((0, rows - logit_t.shape[0]), (0, 0))), segment.reshape(length, 1), segment.reshape(1, length))


MESH = pl.DeviceIdType.MESH
tile = 256
strip = 64


def greet(other):
    barrier = pltpu.get_barrier_semaphore()
    pl.semaphore_signal(barrier, inc=1, device_id={"tensor": other}, device_id_type=MESH)
    pl.semaphore_wait(barrier, 1)


def over(count, body):
    lax.fori_loop(0, count, lambda place, carry: (body(place), carry)[1], 0)


def span(place, size):
    return pl.ds(pl.multiple_of(place * size, size), size)


def to_other(source, target, sends, arrivals, place, other):
    return pltpu.make_async_remote_copy(
        src_ref=source,
        dst_ref=target,
        send_sem=sends.at[place],
        recv_sem=arrivals.at[place],
        device_id={"tensor": other},
        device_id_type=MESH,
    )


def scale_of(rows):
    return lax.rsqrt(jnp.mean(rows * rows, axis=1, keepdims=True) + epsilon)


def strip_copies(held, full, own, far, near, arrivals, place, me, other):
    half = held.shape[0]
    rows = span(place, strip)
    into = pl.ds(pl.multiple_of(me * half + place * strip, strip), strip)
    remote = to_other(held.at[rows], full.at[into], far, arrivals, place, other)
    return remote, pltpu.make_async_copy(held.at[rows], full.at[into], near.at[place])


def gather_body(token_ref, gain_ref, full_ref, held, far, near, arrivals):
    me = lax.axis_index("tensor")
    other = 1 - me
    greet(other)
    count = held.shape[0] // strip
    copies = lambda place: strip_copies(held, full_ref, me, far, near, arrivals, place, me, other)

    def step(place):
        rows = span(place, strip)
        values = token_ref[rows, :].astype(jnp.float32)
        held[rows, :] = (values * scale_of(values) * gain_ref[...]).astype(low)
        for copy in copies(place):
            copy.start()

    over(count, step)

    def finish(place):
        for copy in copies(place):
            copy.wait()

    over(count, finish)


def exchange_products(product, send, recv, total, sends, arrivals, me, other):
    half = total.shape[0]
    count = total.shape[1] // tile
    copy = lambda place: to_other(send.at[place], recv.at[place], sends, arrivals, place, other)

    def away(place):
        send[place] = product(span(other, half), place).astype(low)
        copy(place).start()

    def home(place):
        columns = span(place, tile)
        total[:, columns] = product(span(me, half), place)
        copy(place).wait()
        total[:, columns] += recv[place].astype(jnp.float32)

    over(count, away)
    over(count, home)


def project_body(gated_ref, weight_ref, token_ref, cot_ref, gain_ref, middle_ref, full_ref, up_ref, send, recv, held, sends, arrivals, far, near, landed, up_sems):
    me = lax.axis_index("tensor")
    other = 1 - me
    greet(other)
    half = token_ref.shape[0]
    up_far = pltpu.make_async_remote_copy(
        src_ref=cot_ref, dst_ref=up_ref.at[span(me, half)], send_sem=up_sems.at[0], recv_sem=up_sems.at[1],
        device_id={"tensor": other}, device_id_type=MESH,
    )
    up_near = pltpu.make_async_copy(cot_ref, up_ref.at[span(me, half)], up_sems.at[2])
    up_near.start()

    def product(rows, place):
        return jnp.dot(gated_ref[rows, :], weight_ref[:, span(place, tile)], preferred_element_type=jnp.float32)

    exchange_products(product, send, recv, middle_ref, sends, arrivals, me, other)
    up_far.start()
    count = half // strip
    copies = lambda place: strip_copies(held, full_ref, me, far, near, landed, place, me, other)

    def step(place):
        rows = span(place, strip)
        middle = token_ref[rows, :].astype(jnp.float32) + middle_ref[rows, :]
        middle_ref[rows, :] = middle
        held[rows, :] = (middle * scale_of(middle) * gain_ref[...]).astype(low)
        for copy in copies(place):
            copy.start()

    over(count, step)

    def finish(place):
        for copy in copies(place):
            copy.wait()

    over(count, finish)
    up_near.wait()
    up_far.wait()


def result_body(hidden_ref, weight_ref, middle_ref, result_ref, send, recv, total, sends, arrivals):
    me = lax.axis_index("tensor")
    other = 1 - me
    greet(other)

    def product(rows, place):
        return jnp.dot(hidden_ref[rows, :], weight_ref[:, span(place, tile)], preferred_element_type=jnp.float32)

    exchange_products(product, send, recv, total, sends, arrivals, me, other)

    def step(place):
        rows = span(place, strip)
        result_ref[rows, :] = (total[rows, :] + middle_ref[rows, :]).astype(low)

    over(total.shape[0] // strip, step)


def nt(former, latter):
    return lax.dot_general(former, latter, (((1,), (1,)), ((), ())), preferred_element_type=jnp.float32)


def back_body(gate_ref, up_ref, gate_weight_ref, up_weight_ref, middle_ref, cot_ref, gain_ref, out_ref, full_ref, part_ref, send, recv, total, held, sends, arrivals, far, near, landed):
    me = lax.axis_index("tensor")
    other = 1 - me
    greet(other)

    def product(rows, place):
        columns = span(place, tile)
        return nt(gate_ref[rows, :], gate_weight_ref[columns, :]) + nt(up_ref[rows, :], up_weight_ref[columns, :])

    exchange_products(product, send, recv, total, sends, arrivals, me, other)
    part_ref[...] = jnp.zeros_like(part_ref)
    count = total.shape[0] // strip
    copies = lambda place: strip_copies(held, full_ref, me, far, near, landed, place, me, other)

    def step(place):
        rows = span(place, strip)
        middle = middle_ref[rows, :]
        scale = scale_of(middle)
        normed = middle * scale
        upstream = total[rows, :]
        weighted = upstream * gain_ref[...]
        push = scale * (weighted - normed * jnp.mean(weighted * normed, axis=1, keepdims=True))
        grad = cot_ref[rows, :].astype(jnp.float32) + push
        out_ref[rows, :] = grad
        held[rows, :] = grad.astype(low)
        for copy in copies(place):
            copy.start()
        part_ref[...] += jnp.sum((upstream * normed).reshape(strip // 8, 8, -1), axis=0)

    over(count, step)

    def finish(place):
        for copy in copies(place):
            copy.wait()

    over(count, finish)


def first_body(query_ref, key_ref, value_ref, gate_ref, forget_ref, wq_ref, wk_ref, wv_ref, wg_ref, wf_ref, grad_ref, token_ref, gain_ref, out_ref, part_ref, send, recv, total, sends, arrivals):
    me = lax.axis_index("tensor")
    other = 1 - me
    greet(other)

    def product(rows, place):
        columns = span(place, tile)
        value = nt(query_ref[rows, :], wq_ref[columns, :]) + nt(key_ref[rows, :], wk_ref[columns, :])
        value = value + nt(value_ref[rows, :], wv_ref[columns, :]) + nt(gate_ref[rows, :], wg_ref[columns, :])
        return value + lax.dot_general(
            forget_ref[:, rows], wf_ref[:, columns], (((0,), (0,)), ((), ())), preferred_element_type=jnp.float32
        )

    exchange_products(product, send, recv, total, sends, arrivals, me, other)
    part_ref[...] = jnp.zeros_like(part_ref)

    def step(place):
        rows = span(place, strip)
        values = token_ref[rows, :].astype(jnp.float32)
        scale = scale_of(values)
        normed = values * scale
        upstream = total[rows, :]
        weighted = upstream * gain_ref[...]
        push = scale * (weighted - normed * jnp.mean(weighted * normed, axis=1, keepdims=True))
        out_ref[rows, :] = grad_ref[rows, :] + push
        part_ref[...] += jnp.sum((upstream * normed).reshape(strip // 8, 8, -1), axis=0)

    over(total.shape[0] // strip, step)


def all_sum_body(bits, part_ref, out_ref, slots, sends, arrivals):
    out_ref[...] = part_ref[...]
    places = {}
    for axis in ("dp", "tensor"):
        places[axis] = lax.axis_index(axis)
    partners = []
    for axis, bit in bits:
        here = places[axis]
        flip = here + (1 << bit) - 2 * (1 << bit) * (here // (1 << bit) % 2)
        partners.append({axis: flip})
    barrier = pltpu.get_barrier_semaphore()
    for partner in partners:
        pl.semaphore_signal(barrier, inc=1, device_id=partner, device_id_type=MESH)
    pl.semaphore_wait(barrier, len(partners))
    for place, partner in enumerate(partners):
        copy = pltpu.make_async_remote_copy(
            src_ref=slots.at[2 * place], dst_ref=slots.at[2 * place + 1], send_sem=sends.at[place],
            recv_sem=arrivals.at[place], device_id=partner, device_id_type=MESH,
        )
        slots[2 * place] = out_ref[...]
        copy.start()
        copy.wait()
        out_ref[...] += slots[2 * place + 1]


vmem = pl.BlockSpec(memory_space=pltpu.VMEM)
anywhere = pl.BlockSpec(memory_space=pl.ANY)
dma = pltpu.SemaphoreType.DMA


def comm_params(identity):
    return pltpu.CompilerParams(collective_id=identity, has_side_effects=True, vmem_limit_bytes=60 * 2**20)


def norm_gather(tokens, gain):
    half, width = tokens.shape
    count = half // strip
    return pl.pallas_call(
        gather_body,
        out_shape=jax.ShapeDtypeStruct((2 * half, width), low),
        in_specs=[vmem, vmem],
        out_specs=anywhere,
        scratch_shapes=[pltpu.VMEM((half, width), low), dma((count,)), dma((count,)), dma((count,))],
        compiler_params=comm_params(0),
        cost_estimate=pl.CostEstimate(flops=8 * half * width, bytes_accessed=12 * half * width, transcendentals=half),
        name="norm_gather",
    )(tokens, gain.reshape(1, width))


def exchange_scratch(half, width):
    count = width // tile
    return [pltpu.VMEM((count, half, tile), low), pltpu.VMEM((count, half, tile), low)], [dma((count,)), dma((count,))]


def project(gated, weight, tokens, cotangent, gain):
    half, width = tokens.shape
    count = half // strip
    buffers, sems = exchange_scratch(half, width)
    return pl.pallas_call(
        project_body,
        out_shape=[
            jax.ShapeDtypeStruct((half, width), jnp.float32),
            jax.ShapeDtypeStruct((2 * half, width), low),
            jax.ShapeDtypeStruct((2 * half, width), low),
        ],
        in_specs=[vmem] * 5,
        out_specs=[vmem, anywhere, anywhere],
        scratch_shapes=buffers + [pltpu.VMEM((half, width), low)] + sems + [dma((count,)), dma((count,)), dma((count,)), dma((3,))],
        compiler_params=comm_params(1),
        cost_estimate=pl.CostEstimate(flops=4 * half * width * weight.shape[0], bytes_accessed=24 * half * width, transcendentals=half),
        name="project",
    )(gated, weight, tokens, cotangent, gain.reshape(1, width))


def result_rows(hidden, weight, middle):
    half, width = middle.shape
    buffers, sems = exchange_scratch(half, width)
    return pl.pallas_call(
        result_body,
        out_shape=jax.ShapeDtypeStruct((half, width), low),
        in_specs=[vmem] * 3,
        out_specs=vmem,
        scratch_shapes=buffers + [pltpu.VMEM((half, width), jnp.float32)] + sems,
        compiler_params=comm_params(2),
        cost_estimate=pl.CostEstimate(flops=4 * half * width * weight.shape[0], bytes_accessed=30 * half * width, transcendentals=0),
        name="result_rows",
    )(hidden, weight, middle)


def middle_back(gate_grad, up_grad, gate_weight, up_weight, middle, cotangent, gain):
    half, width = middle.shape
    count = half // strip
    buffers, sems = exchange_scratch(half, width)
    return pl.pallas_call(
        back_body,
        out_shape=[
            jax.ShapeDtypeStruct((half, width), jnp.float32),
            jax.ShapeDtypeStruct((2 * half, width), low),
            jax.ShapeDtypeStruct((8, width), jnp.float32),
        ],
        in_specs=[vmem] * 7,
        out_specs=[vmem, anywhere, vmem],
        scratch_shapes=buffers
        + [pltpu.VMEM((half, width), jnp.float32), pltpu.VMEM((half, width), low)]
        + sems
        + [dma((count,)), dma((count,)), dma((count,))],
        compiler_params=comm_params(3),
        cost_estimate=pl.CostEstimate(flops=8 * half * width * gate_weight.shape[1], bytes_accessed=50 * half * width, transcendentals=half),
        name="middle_back",
    )(gate_grad, up_grad, gate_weight, up_weight, middle, cotangent, gain.reshape(1, width))


def first_back(query_grad, key_grad, value_grad, outgate_grad, forget_grad, weights, forget_t, middle_grad, tokens, gain):
    half, width = tokens.shape
    buffers, sems = exchange_scratch(half, width)
    return pl.pallas_call(
        first_body,
        out_shape=[
            jax.ShapeDtypeStruct((half, width), jnp.float32),
            jax.ShapeDtypeStruct((8, width), jnp.float32),
        ],
        in_specs=[vmem] * 13,
        out_specs=[vmem, vmem],
        scratch_shapes=buffers + [pltpu.VMEM((half, width), jnp.float32)] + sems,
        compiler_params=comm_params(4),
        cost_estimate=pl.CostEstimate(flops=16 * half * width * query_grad.shape[1], bytes_accessed=40 * half * width, transcendentals=half),
        name="first_back",
    )(query_grad, key_grad, value_grad, outgate_grad, forget_grad, *weights, forget_t, middle_grad, tokens, gain.reshape(1, width))


def all_sum(part):
    bits = [("tensor", bit) for bit in range(lax.axis_size("tensor").bit_length() - 1)]
    bits += [("dp", bit) for bit in range(lax.axis_size("dp").bit_length() - 1)]
    return pl.pallas_call(
        partial(all_sum_body, bits),
        out_shape=jax.ShapeDtypeStruct(part.shape, part.dtype),
        in_specs=[vmem],
        out_specs=vmem,
        scratch_shapes=[pltpu.VMEM((2 * len(bits),) + part.shape, part.dtype), dma((len(bits),)), dma((len(bits),))],
        compiler_params=comm_params(5),
        name="all_sum",
    )(part)


def local(
    tokens,
    segment_ids,
    first_gain,
    query_weight,
    key_weight,
    value_weight,
    outgate_weight,
    forget_weight,
    forget_bias,
    output_weight,
    second_gain,
    gate_weight,
    up_weight,
    down_weight,
    cotangent,
):
    local_heads = forget_weight.shape[1]
    head_dim = query_weight.shape[1] // local_heads
    paired = lax.axis_size("tensor") == 2
    segment = segment_ids[0]
    gather = partial(lax.all_gather, axis_name="tensor", axis=0, tiled=True)
    scatter = partial(lax.psum_scatter, axis_name="tensor", scatter_dimension=0, tiled=True)

    if paired:
        first_all = norm_gather(tokens, first_gain)
    else:
        inputs = tokens.astype(jnp.float32)
        scale_one = norm_scale(inputs)
        normed_one = inputs * scale_one
        first_all = gather((normed_one * first_gain).astype(low))
    query_rows = matmul(first_all, query_weight).astype(low)
    key_rows = matmul(first_all, key_weight).astype(low)
    value_rows = matmul(first_all, value_weight).astype(low)
    outgate = jax.nn.sigmoid(matmul(first_all, outgate_weight))
    logit_t = lax.dot_general(
        forget_weight, first_all, (((0,), (1,)), ((), ())), preferred_element_type=jnp.float32
    ) + forget_bias[:, None]
    mixed_out, gated_out, peaks = attend_forward(
        query_rows, key_rows, value_rows, outgate, logit_t, segment, head_dim
    )
    if paired:
        middle, second_all, upstream = project(gated_out, output_weight, tokens, cotangent, second_gain)
    else:
        middle = inputs + scatter(matmul(gated_out, output_weight))
        scale_two = norm_scale(middle)
        normed_two = middle * scale_two
        second_all = gather((normed_two * second_gain).astype(low))
        upstream = gather(cotangent)
    gate_pre = matmul(second_all, gate_weight)
    up_pre = matmul(second_all, up_weight)
    sigmoid_gate = jax.nn.sigmoid(gate_pre)
    swish_out = gate_pre * sigmoid_gate
    hidden = (swish_out * up_pre).astype(low)
    along, across, deep = (), ((0, 1),), ((0, 2),)
    half = hidden.shape[1] // 2
    down_front = inner_rows(upstream, hidden[:, :half]).astype(low)
    down_back = inner_rows(upstream, hidden[:, half:]).astype(low)
    hidden_grad = against(upstream, down_weight)
    gate_grad = (
        hidden_grad * up_pre * sigmoid_gate * (1.0 + gate_pre * (1.0 - sigmoid_gate))
    ).astype(low)
    up_grad = (hidden_grad * swish_out).astype(low)
    gate_grad, up_grad, down_front, down_back = lax.optimization_barrier(
        (gate_grad, up_grad, down_front, down_back)
    )
    grad_gate = inner_rows(second_all, gate_grad).astype(low)
    grad_up = inner_rows(second_all, up_grad).astype(low)
    gate_grad, up_grad, grad_gate, grad_up = lax.optimization_barrier(
        (gate_grad, up_grad, grad_gate, grad_up)
    )
    if paired:
        middle_grad, middle_all, gain_two_part = middle_back(
            gate_grad, up_grad, gate_weight, up_weight, middle, cotangent, second_gain
        )
    else:
        second_grad = scatter(against(gate_grad, gate_weight) + against(up_grad, up_weight))
        middle_grad = cotangent.astype(jnp.float32) + norm_back(
            second_grad, normed_two, scale_two, second_gain
        )
        gain_two_part = jnp.sum(second_grad * normed_two, axis=0, keepdims=True)
        middle_all = gather(middle_grad.astype(low))
    grad_output = inner_rows(middle_all, gated_out).astype(low)
    gated_grad = against(middle_all, output_weight)
    mixed_grad = (gated_grad * outgate).astype(low)
    outgate_grad = (gated_grad * mixed_out * outgate * (1.0 - outgate)).astype(low)
    grad_outgate = inner_rows(first_all, outgate_grad).astype(low)
    mixed_grad, grad_output, grad_outgate = lax.optimization_barrier(
        (mixed_grad, grad_output, grad_outgate)
    )
    query_grad, key_grad, value_grad, forget_rows = attend_backward(
        query_rows, key_rows, value_rows, mixed_grad, peaks, logit_t, segment, head_dim
    )
    grad_query = inner_rows(first_all, query_grad).astype(low)
    grad_key = inner_rows(first_all, key_grad).astype(low)
    grad_value = inner_rows(first_all, value_grad).astype(low)
    forget_grad = forget_rows[:local_heads]
    grad_forget = lax.dot_general(
        first_all, forget_grad, (((0,), (1,)), ((), ())), preferred_element_type=jnp.float32
    ).astype(low)
    bias_part = jnp.sum(forget_grad.astype(jnp.float32), axis=1)
    forget_t = forget_weight.T
    if paired:
        forget_t = jnp.pad(forget_t, ((0, forget_rows.shape[0] - local_heads), (0, 0)))
        weights = (query_weight, key_weight, value_weight, outgate_weight)
        tokens_grad, gain_one_part = first_back(
            query_grad, key_grad, value_grad, outgate_grad, forget_rows, weights, forget_t,
            middle_grad, tokens, first_gain,
        )
    else:
        total = against(query_grad, query_weight)
        total = total + against(key_grad, key_weight)
        total = total + against(value_grad, value_weight)
        total = total + against(outgate_grad, outgate_weight)
        total = total + inner_rows(forget_grad, forget_t)
        first_grad = scatter(total.astype(low)).astype(jnp.float32)
        tokens_grad = middle_grad + norm_back(first_grad, normed_one, scale_one, first_gain)
        gain_one_part = jnp.sum(first_grad * normed_one, axis=0, keepdims=True)
    all_heads = local_heads * lax.axis_size("tensor")
    placed = lax.dynamic_update_slice(
        jnp.zeros((1, tokens.shape[1]), jnp.float32),
        bias_part[None],
        (0, lax.axis_index("tensor") * local_heads),
    )
    shares = jnp.concatenate(
        [
            jnp.sum(gain_one_part, axis=0, keepdims=True),
            jnp.sum(gain_two_part, axis=0, keepdims=True),
            placed,
            jnp.zeros((5, tokens.shape[1]), jnp.float32),
        ]
    )
    sums = all_sum(shares)
    width = grad_query.shape[1]
    query_part = spread_sum(jnp.concatenate([grad_query, grad_forget], axis=1), along)
    return (
        result_rows(hidden, down_weight, middle)
        if paired
        else (middle + scatter(matmul(hidden, down_weight).astype(low)).astype(jnp.float32)).astype(low),
        tokens_grad,
        sums[0],
        query_part[:, :width],
        spread_sum(grad_key, across),
        spread_sum(grad_value, deep),
        spread_sum(grad_outgate, across),
        query_part[:, width:],
        sums[2, :all_heads],
        spread_sum(grad_output, along).T,
        sums[1],
        spread_sum(grad_gate, along),
        spread_sum(grad_up, across),
        jnp.concatenate([spread_sum(down_front, along), spread_sum(down_back, across)], axis=1).T,
    )


def solution(mesh):
    in_specs = (
        P(("dp", "tensor"), None),
        P("dp", None),
        P(),
        P(None, "tensor"),
        P(None, "tensor"),
        P(None, "tensor"),
        P(None, "tensor"),
        P(None, "tensor"),
        P("tensor"),
        P("tensor", None),
        P(),
        P(None, "tensor"),
        P(None, "tensor"),
        P("tensor", None),
        P(("dp", "tensor"), None),
    )
    out_specs = (
        P(("dp", "tensor"), None),
        P(("dp", "tensor"), None),
        P(),
        P("dp", "tensor"),
        P("dp", "tensor"),
        P("dp", "tensor"),
        P("dp", "tensor"),
        P("dp", "tensor"),
        P(),
        P("tensor", "dp"),
        P(),
        P("dp", "tensor"),
        P("dp", "tensor"),
        P("tensor", "dp"),
    )
    return jax.shard_map(local, mesh=mesh, in_specs=in_specs, out_specs=out_specs, check_vma=False)
```

```python
from functools import partial

import jax
import jax.numpy as jnp
from jax import lax
from jax.experimental import pallas as pl
from jax.experimental.pallas import tpu as pltpu
from jax.sharding import PartitionSpec as P

epsilon = 1e-06
masked_value = -1e30


def matmul(former, latter):
    return jnp.dot(former, latter, preferred_element_type=jnp.float32)


def inner_rows(former, latter):
    return lax.dot_general(
        former, latter, (((0,), (0,)), ((), ())), preferred_element_type=jnp.float32
    )


def against(former, latter):
    return lax.dot_general(
        former, latter, (((1,), (1,)), ((), ())), preferred_element_type=jnp.float32
    )


def norm_scale(matrix):
    return lax.rsqrt(jnp.mean(matrix * matrix, axis=1, keepdims=True) + epsilon)


def norm_back(upstream, normed, scaling, gain_vec):
    weighted = upstream * gain_vec
    return scaling * (weighted - normed * jnp.mean(weighted * normed, axis=1, keepdims=True))


class Flow:
    def __init__(self, gradient, swap):
        self.count = lax.axis_size("dp")
        self.bits = self.count.bit_length() - 1
        self.order = list(range(self.bits))
        for front, back in swap:
            self.order[front], self.order[back] = self.order[back], self.order[front]
        self.live = list(range(self.bits - 1, -1, -1))
        self.whole = gradient.reshape(
            (2,) * self.bits + (gradient.shape[0] // self.count, gradient.shape[1])
        )
        self.stage = 0
        self.cut()

    def cut(self):
        bit = self.order[self.stage]
        axis = self.live.index(bit)
        self.live.pop(axis)
        mine = (lax.axis_index("dp") >> bit) & 1
        self.sent = lax.dynamic_index_in_dim(self.whole, 1 - mine, axis, keepdims=False)
        self.kept = lax.dynamic_index_in_dim(self.whole, mine, axis, keepdims=False)

    def fly(self):
        bit = self.order[self.stage]
        pairs = [(place, place ^ (1 << bit)) for place in range(self.count)]
        self.got = lax.ppermute(self.sent, "dp", pairs)

    def land(self):
        total = self.kept.astype(jnp.float32) + self.got.astype(jnp.float32)
        self.stage += 1
        if self.stage == self.bits:
            self.whole = total
            return
        self.whole = total.astype(jnp.bfloat16)
        self.cut()

    def done(self):
        return self.stage == self.bits


def tie(values, start=(), end=()):
    values, sent, got = lax.optimization_barrier(
        (values, tuple(flow.sent for flow in start), tuple(flow.got for flow in end))
    )
    for flow, one in zip(start, sent):
        flow.sent = one
        flow.fly()
    for flow, one in zip(end, got):
        flow.got = one
        flow.land()
    return values


block_rows = 256
longest_doc = 512
low = jnp.bfloat16
log2e = 1.4426950408889634


def windows(length):
    reach = -(-(longest_doc - 1) // block_rows)
    spans = []
    place = 0
    for one in range(length // block_rows):
        start = max(0, one - reach) * block_rows
        width = (one + 1) * block_rows - start
        spans.append((one * block_rows, start, width, place))
        place += width
    return spans, place


def lane_of(shape):
    return lax.broadcasted_iota(jnp.int32, shape, len(shape) - 1)


def running(rows, back):
    length = rows.shape[1]
    lanes = lane_of(rows.shape)
    step = 1
    while step < length:
        if back:
            moved = jnp.where(lanes < length - step, pltpu.roll(rows, length - step, 1), 0.0)
        else:
            moved = jnp.where(lanes >= step, pltpu.roll(rows, step, 1), 0.0)
        rows = rows + moved
        step *= 2
    return rows


def log_sigmoid(value):
    return jnp.minimum(value, 0.0) - jnp.log1p(jnp.exp(-jnp.abs(value)))


def fill_bias(seg_col, seg_row, bias, spans):
    for first, start, width, place in spans:
        rows = first + lax.broadcasted_iota(jnp.int32, (block_rows, width), 0)
        cols = start + lax.broadcasted_iota(jnp.int32, (block_rows, width), 1)
        same = seg_col[first : first + block_rows, :] == seg_row[:, start : start + width]
        bias[:, place : place + width] = jnp.where((cols <= rows) & same, 0.0, masked_value)


def head_parts(block, head_dim, head, mark):
    lanes = lane_of(block.shape)
    kept = jnp.where(lanes // head_dim == head, block, jnp.zeros_like(block))
    if mark is None:
        return kept
    return jnp.where(lanes == mark, jnp.ones_like(block), kept)


def forward_body(q_ref, k_ref, v_ref, gate_ref, logit_ref, col_ref, row_ref, mixed_ref, gated_ref, peak_ref, bias, fall, *, head_dim, spans, heads):
    pair = pl.program_id(0)

    @pl.when(pair == 0)
    def _():
        fill_bias(col_ref[...], row_ref[...], bias, spans)
        fall[...] = running(log_sigmoid(logit_ref[...]), False) * log2e

    lanes = lane_of((block_rows, q_ref.shape[1]))
    falls = [fall[pl.ds(pair * heads + head, 1), :] for head in range(heads)]
    for first, start, width, place in spans:
        query = q_ref[first : first + block_rows, :]
        key = k_ref[start : start + width, :]
        value = v_ref[start : start + width, :]
        mixed = None
        peaks = None
        for head in range(heads):
            line = falls[head]
            shift = line[:, first : first + 1] - line[:, start : start + width]
            scores = lax.dot_general(
                head_parts(query, head_dim, head, None), key, (((1,), (1,)), ((), ())),
                preferred_element_type=jnp.float32,
            )
            scores = scores * (head_dim**-0.5 * log2e) + shift + bias[:, place : place + width]
            top = jnp.max(scores, axis=1, keepdims=True)
            weight = jnp.exp2(scores - top)
            total = jnp.sum(weight, axis=1, keepdims=True)
            weight = (weight * (1.0 / total)).astype(low)
            part = jnp.dot(weight, head_parts(value, head_dim, head, None), preferred_element_type=jnp.float32)
            peak = jnp.broadcast_to(top + jnp.log2(total), lanes.shape)
            mixed = part if mixed is None else mixed + part
            peaks = peak if peaks is None else jnp.where(lanes // head_dim == head, peak, peaks)
        rows = slice(first, first + block_rows)
        mixed_ref[rows, :] = mixed
        peak_ref[rows, :] = peaks
        gated_ref[rows, :] = (mixed * gate_ref[rows, :]).astype(low)


def attention_sizes(width, head_dim):
    wide = 128 if width % 128 == 0 and 128 % head_dim == 0 else width
    return wide, wide // head_dim


def attend_forward(query, key, value, outgate, logit_t, segment, head_dim):
    length, width = query.shape
    wide, heads = attention_sizes(width, head_dim)
    spans, total = windows(length)
    whole = pl.BlockSpec(memory_space=pltpu.VMEM)
    part = pl.BlockSpec((length, wide), lambda i: (0, i))
    rows = -(-logit_t.shape[0] // 8) * 8
    area = sum(span[2] for span in spans) * block_rows
    return pl.pallas_call(
        partial(forward_body, head_dim=head_dim, spans=spans, heads=heads),
        grid=(width // wide,),
        in_specs=[part, part, part, part, whole, whole, whole],
        out_specs=[part, part, part],
        out_shape=[
            jax.ShapeDtypeStruct((length, width), jnp.float32),
            jax.ShapeDtypeStruct((length, width), low),
            jax.ShapeDtypeStruct((length, width), jnp.float32),
        ],
        scratch_shapes=[
            pltpu.VMEM((block_rows, total), jnp.float32),
            pltpu.VMEM((rows, length), jnp.float32),
        ],
        compiler_params=pltpu.CompilerParams(vmem_limit_bytes=50 * 2**20),
        cost_estimate=pl.CostEstimate(
            flops=16 * area * width, bytes_accessed=20 * length * width, transcendentals=area * width // head_dim
        ),
        name="attend_forward",
    )(query, key, value, outgate, jnp.pad(logit_t, ((0, rows - logit_t.shape[0]), (0, 0))), segment.reshape(length, 1), segment.reshape(1, length))


def backward_body(q_ref, k_ref, v_ref, grad_ref, peak_ref, logit_ref, col_ref, row_ref, dq_ref, dk_ref, dv_ref, forget_ref, bias, fall, key_sum, value_sum, slope, *, head_dim, spans, heads):
    pair = pl.program_id(0)
    wide = q_ref.shape[1]

    @pl.when(pair == 0)
    def _():
        fill_bias(col_ref[...], row_ref[...], bias, spans)
        fall[...] = running(log_sigmoid(logit_ref[...]), False) * log2e
        slope[...] = jnp.zeros_like(slope)

    falls = [fall[pl.ds(pair * heads + head, 1), :] for head in range(heads)]
    scaling = head_dim**-0.5
    value_sum[...] = jnp.zeros_like(value_sum)
    key_sum[...] = jnp.zeros_like(key_sum)
    lanes = lane_of((block_rows, wide))
    slots = lane_of((block_rows, slope.shape[1]))
    marks = [((head + 1) * head_dim) % wide for head in range(heads)]
    for first, start, width, place in spans:
        rows = slice(first, first + block_rows)
        query = q_ref[rows, :]
        key = k_ref[start : start + width, :]
        value = v_ref[start : start + width, :]
        grad = grad_ref[rows, :]
        query_grad = None
        for head in range(heads):
            line = falls[head]
            shift = line[:, first : first + 1] - line[:, start : start + width]
            scores = lax.dot_general(
                head_parts(query, head_dim, head, None), key, (((1,), (1,)), ((), ())),
                preferred_element_type=jnp.float32,
            )
            peak = peak_ref[rows, head * head_dim : head * head_dim + 1]
            scores = scores * (scaling * log2e) + shift + bias[:, place : place + width]
            weight = jnp.exp2(scores - peak)
            own_grad = head_parts(grad, head_dim, head, None)
            rise = lax.dot_general(
                own_grad, value, (((1,), (1,)), ((), ())), preferred_element_type=jnp.float32
            )
            delta = jnp.sum(weight * rise, axis=1, keepdims=True)
            change = (weight * (rise - delta)).astype(low)
            weight = weight.astype(low)
            value_sum[start : start + width, :] += lax.dot_general(
                weight, own_grad, (((0,), (0,)), ((), ())), preferred_element_type=jnp.float32
            )
            mark = marks[head]
            from_key = jnp.dot(change, head_parts(key, head_dim, head, mark), preferred_element_type=jnp.float32)
            key_sum[head, start : start + width, :] += lax.dot_general(
                change, head_parts(query, head_dim, head, mark), (((0,), (0,)), ((), ())),
                preferred_element_type=jnp.float32,
            )
            slope[rows, :] += jnp.where(slots == pair * heads + head, from_key[:, mark : mark + 1], 0.0)
            query_grad = from_key if query_grad is None else jnp.where(lanes // head_dim == head, from_key, query_grad)
        dq_ref[rows, :] = (query_grad * scaling).astype(low)
    length = q_ref.shape[0]
    lanes = lane_of((length, wide))
    slots = lane_of(slope.shape)
    total = key_sum[0]
    gone = jnp.where(slots == pair * heads, total[:, marks[0] : marks[0] + 1], 0.0)
    for head in range(1, heads):
        other = key_sum[head]
        gone += jnp.where(slots == pair * heads + head, other[:, marks[head] : marks[head] + 1], 0.0)
        total = jnp.where(lanes // head_dim == head, other, total)
    slope[...] -= gone
    dk_ref[...] = (total * scaling).astype(low)
    dv_ref[...] = value_sum[...].astype(low)

    @pl.when(pair == pl.num_programs(0) - 1)
    def _():
        count = logit_ref.shape[0]
        turned = slope[...].T[:count, :]
        forget_ref[...] = (running(turned, True) * jax.nn.sigmoid(-logit_ref[...])).astype(low)


def attend_backward(query, key, value, mixed_grad, peaks, logit_t, segment, head_dim):
    length, width = query.shape
    wide, heads = attention_sizes(width, head_dim)
    spans, total = windows(length)
    whole = pl.BlockSpec(memory_space=pltpu.VMEM)
    part = pl.BlockSpec((length, wide), lambda i: (0, i))
    rows = -(-logit_t.shape[0] // 8) * 8
    area = sum(span[2] for span in spans) * block_rows
    return pl.pallas_call(
        partial(backward_body, head_dim=head_dim, spans=spans, heads=heads),
        grid=(width // wide,),
        in_specs=[part, part, part, part, part, whole, whole, whole],
        out_specs=[part, part, part, pl.BlockSpec((rows, length), lambda i: (0, 0))],
        out_shape=[jax.ShapeDtypeStruct((length, width), low)] * 3
        + [jax.ShapeDtypeStruct((rows, length), low)],
        scratch_shapes=[
            pltpu.VMEM((block_rows, total), jnp.float32),
            pltpu.VMEM((rows, length), jnp.float32),
            pltpu.VMEM((heads, length, wide), jnp.float32),
            pltpu.VMEM((length, wide), jnp.float32),
            pltpu.VMEM((length, 128), jnp.float32),
        ],
        compiler_params=pltpu.CompilerParams(vmem_limit_bytes=50 * 2**20),
        cost_estimate=pl.CostEstimate(
            flops=40 * area * width, bytes_accessed=20 * length * width, transcendentals=area * width // head_dim
        ),
        name="attend_backward",
    )(query, key, value, mixed_grad, peaks, jnp.pad(logit_t, ((0, rows - logit_t.shape[0]), (0, 0))), segment.reshape(length, 1), segment.reshape(1, length))


MESH = pl.DeviceIdType.MESH
tile = 256
strip = 64


def greet(other):
    barrier = pltpu.get_barrier_semaphore()
    pl.semaphore_signal(barrier, inc=1, device_id={"tensor": other}, device_id_type=MESH)
    pl.semaphore_wait(barrier, 1)


def over(count, body):
    lax.fori_loop(0, count, lambda place, carry: (body(place), carry)[1], 0)


def span(place, size):
    return pl.ds(pl.multiple_of(place * size, size), size)


def to_other(source, target, sends, arrivals, place, other):
    return pltpu.make_async_remote_copy(
        src_ref=source,
        dst_ref=target,
        send_sem=sends.at[place],
        recv_sem=arrivals.at[place],
        device_id={"tensor": other},
        device_id_type=MESH,
    )


def scale_of(rows):
    return lax.rsqrt(jnp.mean(rows * rows, axis=1, keepdims=True) + epsilon)


def strip_copies(held, full, own, far, near, arrivals, place, me, other):
    half = held.shape[0]
    rows = span(place, strip)
    into = pl.ds(pl.multiple_of(me * half + place * strip, strip), strip)
    remote = to_other(held.at[rows], full.at[into], far, arrivals, place, other)
    return remote, pltpu.make_async_copy(held.at[rows], full.at[into], near.at[place])


def gather_body(token_ref, gain_ref, full_ref, held, far, near, arrivals):
    me = lax.axis_index("tensor")
    other = 1 - me
    greet(other)
    count = held.shape[0] // strip
    copies = lambda place: strip_copies(held, full_ref, me, far, near, arrivals, place, me, other)

    def step(place):
        rows = span(place, strip)
        values = token_ref[rows, :].astype(jnp.float32)
        held[rows, :] = (values * scale_of(values) * gain_ref[...]).astype(low)
        for copy in copies(place):
            copy.start()

    over(count, step)

    def finish(place):
        for copy in copies(place):
            copy.wait()

    over(count, finish)


def exchange_products(product, send, recv, total, sends, arrivals, me, other):
    half = total.shape[0]
    count = total.shape[1] // tile
    copy = lambda place: to_other(send.at[place], recv.at[place], sends, arrivals, place, other)

    def away(place):
        send[place] = product(span(other, half), place).astype(low)
        copy(place).start()

    def home(place):
        columns = span(place, tile)
        total[:, columns] = product(span(me, half), place)
        copy(place).wait()
        total[:, columns] += recv[place].astype(jnp.float32)

    over(count, away)
    over(count, home)


def project_body(gated_ref, weight_ref, token_ref, cot_ref, gain_ref, middle_ref, full_ref, up_ref, send, recv, held, sends, arrivals, far, near, landed, up_sems):
    me = lax.axis_index("tensor")
    other = 1 - me
    greet(other)
    half = token_ref.shape[0]
    up_far = pltpu.make_async_remote_copy(
        src_ref=cot_ref, dst_ref=up_ref.at[span(me, half)], send_sem=up_sems.at[0], recv_sem=up_sems.at[1],
        device_id={"tensor": other}, device_id_type=MESH,
    )
    up_near = pltpu.make_async_copy(cot_ref, up_ref.at[span(me, half)], up_sems.at[2])
    up_near.start()

    def product(rows, place):
        return jnp.dot(gated_ref[rows, :], weight_ref[:, span(place, tile)], preferred_element_type=jnp.float32)

    exchange_products(product, send, recv, middle_ref, sends, arrivals, me, other)
    up_far.start()
    count = half // strip
    copies = lambda place: strip_copies(held, full_ref, me, far, near, landed, place, me, other)

    def step(place):
        rows = span(place, strip)
        middle = token_ref[rows, :].astype(jnp.float32) + middle_ref[rows, :]
        middle_ref[rows, :] = middle
        held[rows, :] = (middle * scale_of(middle) * gain_ref[...]).astype(low)
        for copy in copies(place):
            copy.start()

    over(count, step)

    def finish(place):
        for copy in copies(place):
            copy.wait()

    over(count, finish)
    up_near.wait()
    up_far.wait()


def result_body(hidden_ref, weight_ref, middle_ref, result_ref, send, recv, total, sends, arrivals):
    me = lax.axis_index("tensor")
    other = 1 - me
    greet(other)

    def product(rows, place):
        return jnp.dot(hidden_ref[rows, :], weight_ref[:, span(place, tile)], preferred_element_type=jnp.float32)

    exchange_products(product, send, recv, total, sends, arrivals, me, other)

    def step(place):
        rows = span(place, strip)
        result_ref[rows, :] = (total[rows, :] + middle_ref[rows, :]).astype(low)

    over(total.shape[0] // strip, step)


def nt(former, latter):
    return lax.dot_general(former, latter, (((1,), (1,)), ((), ())), preferred_element_type=jnp.float32)


def back_body(gate_ref, up_ref, gate_weight_ref, up_weight_ref, middle_ref, cot_ref, gain_ref, out_ref, full_ref, part_ref, send, recv, total, held, sends, arrivals, far, near, landed):
    me = lax.axis_index("tensor")
    other = 1 - me
    greet(other)

    def product(rows, place):
        columns = span(place, tile)
        return nt(gate_ref[rows, :], gate_weight_ref[columns, :]) + nt(up_ref[rows, :], up_weight_ref[columns, :])

    exchange_products(product, send, recv, total, sends, arrivals, me, other)
    part_ref[...] = jnp.zeros_like(part_ref)
    count = total.shape[0] // strip
    copies = lambda place: strip_copies(held, full_ref, me, far, near, landed, place, me, other)

    def step(place):
        rows = span(place, strip)
        middle = middle_ref[rows, :]
        scale = scale_of(middle)
        normed = middle * scale
        upstream = total[rows, :]
        weighted = upstream * gain_ref[...]
        push = scale * (weighted - normed * jnp.mean(weighted * normed, axis=1, keepdims=True))
        grad = cot_ref[rows, :].astype(jnp.float32) + push
        out_ref[rows, :] = grad
        held[rows, :] = grad.astype(low)
        for copy in copies(place):
            copy.start()
        part_ref[...] += jnp.sum((upstream * normed).reshape(strip // 8, 8, -1), axis=0)

    over(count, step)

    def finish(place):
        for copy in copies(place):
            copy.wait()

    over(count, finish)


def first_body(query_ref, key_ref, value_ref, gate_ref, forget_ref, wq_ref, wk_ref, wv_ref, wg_ref, wf_ref, grad_ref, token_ref, gain_ref, out_ref, part_ref, send, recv, total, sends, arrivals):
    me = lax.axis_index("tensor")
    other = 1 - me
    greet(other)

    def product(rows, place):
        columns = span(place, tile)
        value = nt(query_ref[rows, :], wq_ref[columns, :]) + nt(key_ref[rows, :], wk_ref[columns, :])
        value = value + nt(value_ref[rows, :], wv_ref[columns, :]) + nt(gate_ref[rows, :], wg_ref[columns, :])
        return value + lax.dot_general(
            forget_ref[:, rows], wf_ref[:, columns], (((0,), (0,)), ((), ())), preferred_element_type=jnp.float32
        )

    exchange_products(product, send, recv, total, sends, arrivals, me, other)
    part_ref[...] = jnp.zeros_like(part_ref)

    def step(place):
        rows = span(place, strip)
        values = token_ref[rows, :].astype(jnp.float32)
        scale = scale_of(values)
        normed = values * scale
        upstream = total[rows, :]
        weighted = upstream * gain_ref[...]
        push = scale * (weighted - normed * jnp.mean(weighted * normed, axis=1, keepdims=True))
        out_ref[rows, :] = grad_ref[rows, :] + push
        part_ref[...] += jnp.sum((upstream * normed).reshape(strip // 8, 8, -1), axis=0)

    over(total.shape[0] // strip, step)


def all_sum_body(bits, part_ref, out_ref, slots, sends, arrivals):
    out_ref[...] = part_ref[...]
    places = {}
    for axis in ("dp", "tensor"):
        places[axis] = lax.axis_index(axis)
    partners = []
    for axis, bit in bits:
        here = places[axis]
        flip = here + (1 << bit) - 2 * (1 << bit) * (here // (1 << bit) % 2)
        partners.append({axis: flip})
    barrier = pltpu.get_barrier_semaphore()
    for partner in partners:
        pl.semaphore_signal(barrier, inc=1, device_id=partner, device_id_type=MESH)
    pl.semaphore_wait(barrier, len(partners))
    for place, partner in enumerate(partners):
        copy = pltpu.make_async_remote_copy(
            src_ref=slots.at[2 * place], dst_ref=slots.at[2 * place + 1], send_sem=sends.at[place],
            recv_sem=arrivals.at[place], device_id=partner, device_id_type=MESH,
        )
        slots[2 * place] = out_ref[...]
        copy.start()
        copy.wait()
        out_ref[...] += slots[2 * place + 1]


vmem = pl.BlockSpec(memory_space=pltpu.VMEM)
anywhere = pl.BlockSpec(memory_space=pl.ANY)
dma = pltpu.SemaphoreType.DMA


def comm_params(identity):
    return pltpu.CompilerParams(collective_id=identity, has_side_effects=True, vmem_limit_bytes=60 * 2**20)


def norm_gather(tokens, gain):
    half, width = tokens.shape
    count = half // strip
    return pl.pallas_call(
        gather_body,
        out_shape=jax.ShapeDtypeStruct((2 * half, width), low),
        in_specs=[vmem, vmem],
        out_specs=anywhere,
        scratch_shapes=[pltpu.VMEM((half, width), low), dma((count,)), dma((count,)), dma((count,))],
        compiler_params=comm_params(0),
        cost_estimate=pl.CostEstimate(flops=8 * half * width, bytes_accessed=12 * half * width, transcendentals=half),
        name="norm_gather",
    )(tokens, gain.reshape(1, width))


def exchange_scratch(half, width):
    count = width // tile
    return [pltpu.VMEM((count, half, tile), low), pltpu.VMEM((count, half, tile), low)], [dma((count,)), dma((count,))]


def project(gated, weight, tokens, cotangent, gain):
    half, width = tokens.shape
    count = half // strip
    buffers, sems = exchange_scratch(half, width)
    return pl.pallas_call(
        project_body,
        out_shape=[
            jax.ShapeDtypeStruct((half, width), jnp.float32),
            jax.ShapeDtypeStruct((2 * half, width), low),
            jax.ShapeDtypeStruct((2 * half, width), low),
        ],
        in_specs=[vmem] * 5,
        out_specs=[vmem, anywhere, anywhere],
        scratch_shapes=buffers + [pltpu.VMEM((half, width), low)] + sems + [dma((count,)), dma((count,)), dma((count,)), dma((3,))],
        compiler_params=comm_params(1),
        cost_estimate=pl.CostEstimate(flops=4 * half * width * weight.shape[0], bytes_accessed=24 * half * width, transcendentals=half),
        name="project",
    )(gated, weight, tokens, cotangent, gain.reshape(1, width))


def result_rows(hidden, weight, middle):
    half, width = middle.shape
    buffers, sems = exchange_scratch(half, width)
    return pl.pallas_call(
        result_body,
        out_shape=jax.ShapeDtypeStruct((half, width), low),
        in_specs=[vmem] * 3,
        out_specs=vmem,
        scratch_shapes=buffers + [pltpu.VMEM((half, width), jnp.float32)] + sems,
        compiler_params=comm_params(2),
        cost_estimate=pl.CostEstimate(flops=4 * half * width * weight.shape[0], bytes_accessed=30 * half * width, transcendentals=0),
        name="result_rows",
    )(hidden, weight, middle)


def middle_back(gate_grad, up_grad, gate_weight, up_weight, middle, cotangent, gain):
    half, width = middle.shape
    count = half // strip
    buffers, sems = exchange_scratch(half, width)
    return pl.pallas_call(
        back_body,
        out_shape=[
            jax.ShapeDtypeStruct((half, width), jnp.float32),
            jax.ShapeDtypeStruct((2 * half, width), low),
            jax.ShapeDtypeStruct((8, width), jnp.float32),
        ],
        in_specs=[vmem] * 7,
        out_specs=[vmem, anywhere, vmem],
        scratch_shapes=buffers
        + [pltpu.VMEM((half, width), jnp.float32), pltpu.VMEM((half, width), low)]
        + sems
        + [dma((count,)), dma((count,)), dma((count,))],
        compiler_params=comm_params(3),
        cost_estimate=pl.CostEstimate(flops=8 * half * width * gate_weight.shape[1], bytes_accessed=50 * half * width, transcendentals=half),
        name="middle_back",
    )(gate_grad, up_grad, gate_weight, up_weight, middle, cotangent, gain.reshape(1, width))


def first_back(query_grad, key_grad, value_grad, outgate_grad, forget_grad, weights, forget_t, middle_grad, tokens, gain):
    half, width = tokens.shape
    buffers, sems = exchange_scratch(half, width)
    return pl.pallas_call(
        first_body,
        out_shape=[
            jax.ShapeDtypeStruct((half, width), jnp.float32),
            jax.ShapeDtypeStruct((8, width), jnp.float32),
        ],
        in_specs=[vmem] * 13,
        out_specs=[vmem, vmem],
        scratch_shapes=buffers + [pltpu.VMEM((half, width), jnp.float32)] + sems,
        compiler_params=comm_params(4),
        cost_estimate=pl.CostEstimate(flops=16 * half * width * query_grad.shape[1], bytes_accessed=40 * half * width, transcendentals=half),
        name="first_back",
    )(query_grad, key_grad, value_grad, outgate_grad, forget_grad, *weights, forget_t, middle_grad, tokens, gain.reshape(1, width))


def all_sum(part):
    bits = [("tensor", bit) for bit in range(lax.axis_size("tensor").bit_length() - 1)]
    bits += [("dp", bit) for bit in range(lax.axis_size("dp").bit_length() - 1)]
    return pl.pallas_call(
        partial(all_sum_body, bits),
        out_shape=jax.ShapeDtypeStruct(part.shape, part.dtype),
        in_specs=[vmem],
        out_specs=vmem,
        scratch_shapes=[pltpu.VMEM((2 * len(bits),) + part.shape, part.dtype), dma((len(bits),)), dma((len(bits),))],
        compiler_params=comm_params(5),
        name="all_sum",
    )(part)


def local(
    tokens,
    segment_ids,
    first_gain,
    query_weight,
    key_weight,
    value_weight,
    outgate_weight,
    forget_weight,
    forget_bias,
    output_weight,
    second_gain,
    gate_weight,
    up_weight,
    down_weight,
    cotangent,
):
    local_heads = forget_weight.shape[1]
    head_dim = query_weight.shape[1] // local_heads
    paired = lax.axis_size("tensor") == 2
    segment = segment_ids[0]
    gather = partial(lax.all_gather, axis_name="tensor", axis=0, tiled=True)
    scatter = partial(lax.psum_scatter, axis_name="tensor", scatter_dimension=0, tiled=True)

    if paired:
        first_all = norm_gather(tokens, first_gain)
    else:
        inputs = tokens.astype(jnp.float32)
        scale_one = norm_scale(inputs)
        normed_one = inputs * scale_one
        first_all = gather((normed_one * first_gain).astype(low))
    query_rows = matmul(first_all, query_weight).astype(low)
    key_rows = matmul(first_all, key_weight).astype(low)
    value_rows = matmul(first_all, value_weight).astype(low)
    outgate = jax.nn.sigmoid(matmul(first_all, outgate_weight))
    logit_t = lax.dot_general(
        forget_weight, first_all, (((0,), (1,)), ((), ())), preferred_element_type=jnp.float32
    ) + forget_bias[:, None]
    mixed_out, gated_out, peaks = attend_forward(
        query_rows, key_rows, value_rows, outgate, logit_t, segment, head_dim
    )
    if paired:
        middle, second_all, upstream = project(gated_out, output_weight, tokens, cotangent, second_gain)
    else:
        middle = inputs + scatter(matmul(gated_out, output_weight))
        scale_two = norm_scale(middle)
        normed_two = middle * scale_two
        second_all = gather((normed_two * second_gain).astype(low))
        upstream = gather(cotangent)
    gate_pre = matmul(second_all, gate_weight)
    up_pre = matmul(second_all, up_weight)
    sigmoid_gate = jax.nn.sigmoid(gate_pre)
    swish_out = gate_pre * sigmoid_gate
    hidden = (swish_out * up_pre).astype(low)
    along, across, deep = (), ((0, 1),), ((0, 2),)
    half = hidden.shape[1] // 2
    hidden_grad = against(upstream, down_weight)
    gate_grad = (
        hidden_grad * up_pre * sigmoid_gate * (1.0 + gate_pre * (1.0 - sigmoid_gate))
    ).astype(low)
    up_grad = (hidden_grad * swish_out).astype(low)
    hidden, gate_grad, up_grad = lax.optimization_barrier((hidden, gate_grad, up_grad))
    down = [
        Flow(inner_rows(upstream, hidden[:, :half]).astype(low), along),
        Flow(inner_rows(upstream, hidden[:, half:]).astype(low), across),
    ]
    gate_grad, up_grad = tie((gate_grad, up_grad), start=down)
    gated = [
        Flow(inner_rows(second_all, gate_grad).astype(low), along),
        Flow(inner_rows(second_all, up_grad).astype(low), across),
    ]
    gate_grad, up_grad = tie((gate_grad, up_grad), start=gated, end=down)
    gate_grad, up_grad = tie((gate_grad, up_grad), start=down)
    if paired:
        middle_grad, middle_all, gain_two_part = middle_back(
            gate_grad, up_grad, gate_weight, up_weight, middle, cotangent, second_gain
        )
    else:
        second_grad = scatter(against(gate_grad, gate_weight) + against(up_grad, up_weight))
        middle_grad = cotangent.astype(jnp.float32) + norm_back(
            second_grad, normed_two, scale_two, second_gain
        )
        gain_two_part = jnp.sum(second_grad * normed_two, axis=0, keepdims=True)
        middle_all = gather(middle_grad.astype(low))
    middle_all, outgate = tie((middle_all, outgate), end=down)
    middle_all, outgate = tie((middle_all, outgate), start=down)
    gated_grad = against(middle_all, output_weight)
    mixed_grad = (gated_grad * outgate).astype(low)
    outgate_grad = (gated_grad * mixed_out * outgate * (1.0 - outgate)).astype(low)
    width = query_weight.shape[1]
    shared = Flow(
        jnp.concatenate(
            [inner_rows(middle_all, gated_out).astype(low), inner_rows(first_all, outgate_grad).astype(low)],
            axis=1,
        ),
        deep,
    )
    mixed_grad = tie(mixed_grad, start=[shared])
    query_grad, key_grad, value_grad, forget_rows = attend_backward(
        query_rows, key_rows, value_rows, mixed_grad, peaks, logit_t, segment, head_dim
    )
    query_grad, key_grad, value_grad, forget_rows = tie(
        (query_grad, key_grad, value_grad, forget_rows), end=down + gated
    )
    query_grad, key_grad, value_grad, forget_rows = tie(
        (query_grad, key_grad, value_grad, forget_rows), start=down + gated
    )
    forget_grad = forget_rows[:local_heads]
    grad_forget = lax.dot_general(
        first_all, forget_grad, (((0,), (1,)), ((), ())), preferred_element_type=jnp.float32
    )
    inward = [
        Flow(
            jnp.concatenate([inner_rows(first_all, query_grad).astype(low), grad_forget.astype(low)], axis=1),
            along,
        ),
        Flow(inner_rows(first_all, key_grad).astype(low), across),
        Flow(inner_rows(first_all, value_grad).astype(low), deep),
    ]
    query_grad, hidden = tie((query_grad, hidden), start=inward)
    if paired:
        result = result_rows(hidden, down_weight, middle)
    else:
        rows = scatter(matmul(hidden, down_weight).astype(low)).astype(jnp.float32)
        result = (middle + rows).astype(low)
    result, query_grad = tie((result, query_grad), end=gated + [shared])
    query_grad = tie(query_grad, start=gated + [shared])
    bias_part = jnp.sum(forget_grad.astype(jnp.float32), axis=1)
    forget_t = forget_weight.T
    if paired:
        forget_t = jnp.pad(forget_t, ((0, forget_rows.shape[0] - local_heads), (0, 0)))
        weights = (query_weight, key_weight, value_weight, outgate_weight)
        tokens_grad, gain_one_part = first_back(
            query_grad, key_grad, value_grad, outgate_grad, forget_rows, weights, forget_t,
            middle_grad, tokens, first_gain,
        )
    else:
        total = against(query_grad, query_weight)
        total = total + against(key_grad, key_weight)
        total = total + against(value_grad, value_weight)
        total = total + against(outgate_grad, outgate_weight)
        total = total + inner_rows(forget_grad, forget_t)
        first_grad = scatter(total.astype(low)).astype(jnp.float32)
        tokens_grad = middle_grad + norm_back(first_grad, normed_one, scale_one, first_gain)
        gain_one_part = jnp.sum(first_grad * normed_one, axis=0, keepdims=True)
    all_heads = local_heads * lax.axis_size("tensor")
    placed = lax.dynamic_update_slice(
        jnp.zeros((1, tokens.shape[1]), jnp.float32),
        bias_part[None],
        (0, lax.axis_index("tensor") * local_heads),
    )
    shares = jnp.concatenate(
        [
            jnp.sum(gain_one_part, axis=0, keepdims=True),
            jnp.sum(gain_two_part, axis=0, keepdims=True),
            placed,
            jnp.zeros((5, tokens.shape[1]), jnp.float32),
        ]
    )
    live = down + gated + [shared] + inward
    tokens_grad, shares = tie((tokens_grad, shares), end=live)
    first = True
    while live:
        live = [flow for flow in live if not flow.done()]
        if not live:
            break
        shares = tie(shares, start=live)
        if first:
            sums = all_sum(shares)
            shares = sums
            first = False
        shares = tie(shares, end=live)
    sums = shares
    query_part, shared_part = inward[0].whole, shared.whole
    return (
        result,
        tokens_grad,
        sums[0],
        query_part[:, :width],
        inward[1].whole,
        inward[2].whole,
        shared_part[:, width:],
        query_part[:, width:],
        sums[2, :all_heads],
        shared_part[:, :width].T,
        sums[1],
        gated[0].whole,
        gated[1].whole,
        jnp.concatenate([down[0].whole, down[1].whole], axis=1).T,
    )


def solution(mesh):
    in_specs = (
        P(("dp", "tensor"), None),
        P("dp", None),
        P(),
        P(None, "tensor"),
        P(None, "tensor"),
        P(None, "tensor"),
        P(None, "tensor"),
        P(None, "tensor"),
        P("tensor"),
        P("tensor", None),
        P(),
        P(None, "tensor"),
        P(None, "tensor"),
        P("tensor", None),
        P(("dp", "tensor"), None),
    )
    out_specs = (
        P(("dp", "tensor"), None),
        P(("dp", "tensor"), None),
        P(),
        P("dp", "tensor"),
        P("dp", "tensor"),
        P("dp", "tensor"),
        P("dp", "tensor"),
        P("dp", "tensor"),
        P(),
        P("tensor", "dp"),
        P(),
        P("dp", "tensor"),
        P("dp", "tensor"),
        P("tensor", "dp"),
    )
    return jax.shard_map(local, mesh=mesh, in_specs=in_specs, out_specs=out_specs, check_vma=False)
```

```python
from functools import partial

import jax
import jax.numpy as jnp
from jax import lax
from jax.experimental import pallas as pl
from jax.experimental.pallas import tpu as pltpu
from jax.sharding import PartitionSpec as P

epsilon = 1e-06
masked_value = -1e30


def matmul(former, latter):
    return jnp.dot(former, latter, preferred_element_type=jnp.float32)


def inner_rows(former, latter):
    return lax.dot_general(
        former, latter, (((0,), (0,)), ((), ())), preferred_element_type=jnp.float32
    )


def against(former, latter):
    return lax.dot_general(
        former, latter, (((1,), (1,)), ((), ())), preferred_element_type=jnp.float32
    )


def norm_scale(matrix):
    return lax.rsqrt(jnp.mean(matrix * matrix, axis=1, keepdims=True) + epsilon)


def norm_back(upstream, normed, scaling, gain_vec):
    weighted = upstream * gain_vec
    return scaling * (weighted - normed * jnp.mean(weighted * normed, axis=1, keepdims=True))


class Flow:
    def __init__(self, gradient, swap):
        self.count = lax.axis_size("dp")
        self.bits = self.count.bit_length() - 1
        self.order = list(range(self.bits))
        for front, back in swap:
            self.order[front], self.order[back] = self.order[back], self.order[front]
        self.live = list(range(self.bits - 1, -1, -1))
        gradients = gradient if isinstance(gradient, list) else [gradient]
        self.wholes = [
            one.reshape((2,) * self.bits + (one.shape[0] // self.count, one.shape[1]))
            for one in gradients
        ]
        self.stage = 0
        self.cut()

    def cut(self):
        bit = self.order[self.stage]
        axis = self.live.index(bit)
        self.live.pop(axis)
        mine = (lax.axis_index("dp") >> bit) & 1
        pick = lambda side: jnp.concatenate(
            [lax.dynamic_index_in_dim(one, side, axis, keepdims=False) for one in self.wholes], axis=-1
        )
        self.sent, self.kept = pick(1 - mine), pick(mine)

    def fly(self):
        bit = self.order[self.stage]
        pairs = [(place, place ^ (1 << bit)) for place in range(self.count)]
        self.got = lax.ppermute(self.sent, "dp", pairs)

    def land(self):
        total = self.kept.astype(jnp.float32) + self.got.astype(jnp.float32)
        self.stage += 1
        if self.stage == self.bits:
            self.whole = total
            return
        self.wholes = [total.astype(jnp.bfloat16)]
        self.cut()

    def done(self):
        return self.stage == self.bits


def merged(flows):
    front = flows[0]
    front.sent = jnp.concatenate([flow.sent for flow in flows], axis=-1)
    front.kept = jnp.concatenate([flow.kept for flow in flows], axis=-1)
    return front


def tie(values, start=(), end=()):
    values, sent, got = lax.optimization_barrier(
        (values, tuple(flow.sent for flow in start), tuple(flow.got for flow in end))
    )
    for flow, one in zip(start, sent):
        flow.sent = one
        flow.fly()
    for flow, one in zip(end, got):
        flow.got = one
        flow.land()
    return values


block_rows = 256
longest_doc = 512
low = jnp.bfloat16
log2e = 1.4426950408889634


def windows(length):
    reach = -(-(longest_doc - 1) // block_rows)
    spans = []
    place = 0
    for one in range(length // block_rows):
        start = max(0, one - reach) * block_rows
        width = (one + 1) * block_rows - start
        spans.append((one * block_rows, start, width, place))
        place += width
    return spans, place


def lane_of(shape):
    return lax.broadcasted_iota(jnp.int32, shape, len(shape) - 1)


def running(rows, back):
    length = rows.shape[1]
    lanes = lane_of(rows.shape)
    step = 1
    while step < length:
        if back:
            moved = jnp.where(lanes < length - step, pltpu.roll(rows, length - step, 1), 0.0)
        else:
            moved = jnp.where(lanes >= step, pltpu.roll(rows, step, 1), 0.0)
        rows = rows + moved
        step *= 2
    return rows


def log_sigmoid(value):
    return jnp.minimum(value, 0.0) - jnp.log1p(jnp.exp(-jnp.abs(value)))


def fill_bias(seg_col, seg_row, bias, spans):
    for first, start, width, place in spans:
        rows = first + lax.broadcasted_iota(jnp.int32, (block_rows, width), 0)
        cols = start + lax.broadcasted_iota(jnp.int32, (block_rows, width), 1)
        same = seg_col[first : first + block_rows, :] == seg_row[:, start : start + width]
        bias[:, place : place + width] = jnp.where((cols <= rows) & same, 0.0, masked_value)


def head_parts(block, head_dim, head, mark):
    lanes = lane_of(block.shape)
    kept = jnp.where(lanes // head_dim == head, block, jnp.zeros_like(block))
    if mark is None:
        return kept
    return jnp.where(lanes == mark, jnp.ones_like(block), kept)


def forward_body(q_ref, k_ref, v_ref, gate_ref, logit_ref, col_ref, row_ref, mixed_ref, gated_ref, peak_ref, bias, fall, *, head_dim, spans, heads):
    pair = pl.program_id(0)

    @pl.when(pair == 0)
    def _():
        fill_bias(col_ref[...], row_ref[...], bias, spans)
        fall[...] = running(log_sigmoid(logit_ref[...]), False) * log2e

    lanes = lane_of((block_rows, q_ref.shape[1]))
    falls = [fall[pl.ds(pair * heads + head, 1), :] for head in range(heads)]
    for first, start, width, place in spans:
        query = q_ref[first : first + block_rows, :]
        key = k_ref[start : start + width, :]
        value = v_ref[start : start + width, :]
        mixed = None
        peaks = None
        for head in range(heads):
            line = falls[head]
            shift = line[:, first : first + 1] - line[:, start : start + width]
            scores = lax.dot_general(
                head_parts(query, head_dim, head, None), key, (((1,), (1,)), ((), ())),
                preferred_element_type=jnp.float32,
            )
            scores = scores * (head_dim**-0.5 * log2e) + shift + bias[:, place : place + width]
            top = jnp.max(scores, axis=1, keepdims=True)
            weight = jnp.exp2(scores - top)
            total = jnp.sum(weight, axis=1, keepdims=True)
            weight = (weight * (1.0 / total)).astype(low)
            part = jnp.dot(weight, head_parts(value, head_dim, head, None), preferred_element_type=jnp.float32)
            peak = jnp.broadcast_to(top + jnp.log2(total), lanes.shape)
            mixed = part if mixed is None else mixed + part
            peaks = peak if peaks is None else jnp.where(lanes // head_dim == head, peak, peaks)
        rows = slice(first, first + block_rows)
        mixed_ref[rows, :] = mixed
        peak_ref[rows, :] = peaks
        gated_ref[rows, :] = (mixed * gate_ref[rows, :]).astype(low)


def attention_sizes(width, head_dim):
    wide = 128 if width % 128 == 0 and 128 % head_dim == 0 else width
    return wide, wide // head_dim


def attend_forward(query, key, value, outgate, logit_t, segment, head_dim):
    length, width = query.shape
    wide, heads = attention_sizes(width, head_dim)
    spans, total = windows(length)
    whole = pl.BlockSpec(memory_space=pltpu.VMEM)
    part = pl.BlockSpec((length, wide), lambda i: (0, i))
    rows = -(-logit_t.shape[0] // 8) * 8
    area = sum(span[2] for span in spans) * block_rows
    return pl.pallas_call(
        partial(forward_body, head_dim=head_dim, spans=spans, heads=heads),
        grid=(width // wide,),
        in_specs=[part, part, part, part, whole, whole, whole],
        out_specs=[part, part, part],
        out_shape=[
            jax.ShapeDtypeStruct((length, width), jnp.float32),
            jax.ShapeDtypeStruct((length, width), low),
            jax.ShapeDtypeStruct((length, width), jnp.float32),
        ],
        scratch_shapes=[
            pltpu.VMEM((block_rows, total), jnp.float32),
            pltpu.VMEM((rows, length), jnp.float32),
        ],
        compiler_params=pltpu.CompilerParams(vmem_limit_bytes=50 * 2**20),
        cost_estimate=pl.CostEstimate(
            flops=16 * area * width, bytes_accessed=20 * length * width, transcendentals=area * width // head_dim
        ),
        name="attend_forward",
    )(query, key, value, outgate, jnp.pad(logit_t, ((0, rows - logit_t.shape[0]), (0, 0))), segment.reshape(length, 1), segment.reshape(1, length))


def backward_body(q_ref, k_ref, v_ref, grad_ref, peak_ref, logit_ref, col_ref, row_ref, dq_ref, dk_ref, dv_ref, forget_ref, bias, fall, key_sum, value_sum, slope, *, head_dim, spans, heads):
    pair = pl.program_id(0)
    wide = q_ref.shape[1]

    @pl.when(pair == 0)
    def _():
        fill_bias(col_ref[...], row_ref[...], bias, spans)
        fall[...] = running(log_sigmoid(logit_ref[...]), False) * log2e
        slope[...] = jnp.zeros_like(slope)

    falls = [fall[pl.ds(pair * heads + head, 1), :] for head in range(heads)]
    scaling = head_dim**-0.5
    value_sum[...] = jnp.zeros_like(value_sum)
    key_sum[...] = jnp.zeros_like(key_sum)
    lanes = lane_of((block_rows, wide))
    slots = lane_of((block_rows, slope.shape[1]))
    marks = [((head + 1) * head_dim) % wide for head in range(heads)]
    for first, start, width, place in spans:
        rows = slice(first, first + block_rows)
        query = q_ref[rows, :]
        key = k_ref[start : start + width, :]
        value = v_ref[start : start + width, :]
        grad = grad_ref[rows, :]
        query_grad = None
        for head in range(heads):
            line = falls[head]
            shift = line[:, first : first + 1] - line[:, start : start + width]
            scores = lax.dot_general(
                head_parts(query, head_dim, head, None), key, (((1,), (1,)), ((), ())),
                preferred_element_type=jnp.float32,
            )
            peak = peak_ref[rows, head * head_dim : head * head_dim + 1]
            scores = scores * (scaling * log2e) + shift + bias[:, place : place + width]
            weight = jnp.exp2(scores - peak)
            own_grad = head_parts(grad, head_dim, head, None)
            rise = lax.dot_general(
                own_grad, value, (((1,), (1,)), ((), ())), preferred_element_type=jnp.float32
            )
            delta = jnp.sum(weight * rise, axis=1, keepdims=True)
            change = (weight * (rise - delta)).astype(low)
            weight = weight.astype(low)
            value_sum[start : start + width, :] += lax.dot_general(
                weight, own_grad, (((0,), (0,)), ((), ())), preferred_element_type=jnp.float32
            )
            mark = marks[head]
            from_key = jnp.dot(change, head_parts(key, head_dim, head, mark), preferred_element_type=jnp.float32)
            key_sum[head, start : start + width, :] += lax.dot_general(
                change, head_parts(query, head_dim, head, mark), (((0,), (0,)), ((), ())),
                preferred_element_type=jnp.float32,
            )
            slope[rows, :] += jnp.where(slots == pair * heads + head, from_key[:, mark : mark + 1], 0.0)
            query_grad = from_key if query_grad is None else jnp.where(lanes // head_dim == head, from_key, query_grad)
        dq_ref[rows, :] = (query_grad * scaling).astype(low)
    length = q_ref.shape[0]
    lanes = lane_of((length, wide))
    slots = lane_of(slope.shape)
    total = key_sum[0]
    gone = jnp.where(slots == pair * heads, total[:, marks[0] : marks[0] + 1], 0.0)
    for head in range(1, heads):
        other = key_sum[head]
        gone += jnp.where(slots == pair * heads + head, other[:, marks[head] : marks[head] + 1], 0.0)
        total = jnp.where(lanes // head_dim == head, other, total)
    slope[...] -= gone
    dk_ref[...] = (total * scaling).astype(low)
    dv_ref[...] = value_sum[...].astype(low)

    @pl.when(pair == pl.num_programs(0) - 1)
    def _():
        count = logit_ref.shape[0]
        turned = slope[...].T[:count, :]
        forget_ref[...] = (running(turned, True) * jax.nn.sigmoid(-logit_ref[...])).astype(low)


def attend_backward(query, key, value, mixed_grad, peaks, logit_t, segment, head_dim):
    length, width = query.shape
    wide, heads = attention_sizes(width, head_dim)
    spans, total = windows(length)
    whole = pl.BlockSpec(memory_space=pltpu.VMEM)
    part = pl.BlockSpec((length, wide), lambda i: (0, i))
    rows = -(-logit_t.shape[0] // 8) * 8
    area = sum(span[2] for span in spans) * block_rows
    return pl.pallas_call(
        partial(backward_body, head_dim=head_dim, spans=spans, heads=heads),
        grid=(width // wide,),
        in_specs=[part, part, part, part, part, whole, whole, whole],
        out_specs=[part, part, part, pl.BlockSpec((rows, length), lambda i: (0, 0))],
        out_shape=[jax.ShapeDtypeStruct((length, width), low)] * 3
        + [jax.ShapeDtypeStruct((rows, length), low)],
        scratch_shapes=[
            pltpu.VMEM((block_rows, total), jnp.float32),
            pltpu.VMEM((rows, length), jnp.float32),
            pltpu.VMEM((heads, length, wide), jnp.float32),
            pltpu.VMEM((length, wide), jnp.float32),
            pltpu.VMEM((length, 128), jnp.float32),
        ],
        compiler_params=pltpu.CompilerParams(vmem_limit_bytes=50 * 2**20),
        cost_estimate=pl.CostEstimate(
            flops=40 * area * width, bytes_accessed=20 * length * width, transcendentals=area * width // head_dim
        ),
        name="attend_backward",
    )(query, key, value, mixed_grad, peaks, jnp.pad(logit_t, ((0, rows - logit_t.shape[0]), (0, 0))), segment.reshape(length, 1), segment.reshape(1, length))


MESH = pl.DeviceIdType.MESH
tile = 256
strip = 64


def greet(other):
    barrier = pltpu.get_barrier_semaphore()
    pl.semaphore_signal(barrier, inc=1, device_id={"tensor": other}, device_id_type=MESH)
    pl.semaphore_wait(barrier, 1)


def over(count, body):
    lax.fori_loop(0, count, lambda place, carry: (body(place), carry)[1], 0)


def span(place, size):
    return pl.ds(pl.multiple_of(place * size, size), size)


def to_other(source, target, sends, arrivals, place, other):
    return pltpu.make_async_remote_copy(
        src_ref=source,
        dst_ref=target,
        send_sem=sends.at[place],
        recv_sem=arrivals.at[place],
        device_id={"tensor": other},
        device_id_type=MESH,
    )


def scale_of(rows):
    return lax.rsqrt(jnp.mean(rows * rows, axis=1, keepdims=True) + epsilon)


def strip_copies(held, full, own, far, near, arrivals, place, me, other):
    half = held.shape[0]
    rows = span(place, strip)
    into = pl.ds(pl.multiple_of(me * half + place * strip, strip), strip)
    remote = to_other(held.at[rows], full.at[into], far, arrivals, place, other)
    return remote, pltpu.make_async_copy(held.at[rows], full.at[into], near.at[place])


def gather_body(token_ref, gain_ref, full_ref, held, far, near, arrivals):
    me = lax.axis_index("tensor")
    other = 1 - me
    greet(other)
    count = held.shape[0] // strip
    copies = lambda place: strip_copies(held, full_ref, me, far, near, arrivals, place, me, other)

    def step(place):
        rows = span(place, strip)
        values = token_ref[rows, :].astype(jnp.float32)
        held[rows, :] = (values * scale_of(values) * gain_ref[...]).astype(low)
        for copy in copies(place):
            copy.start()

    over(count, step)

    def finish(place):
        for copy in copies(place):
            copy.wait()

    over(count, finish)


def exchange_products(product, send, recv, total, sends, arrivals, me, other):
    half = total.shape[0]
    count = total.shape[1] // tile
    copy = lambda place: to_other(send.at[place], recv.at[place], sends, arrivals, place, other)

    def away(place):
        send[place] = product(span(other, half), place).astype(low)
        copy(place).start()

    def home(place):
        columns = span(place, tile)
        total[:, columns] = product(span(me, half), place)
        copy(place).wait()
        total[:, columns] += recv[place].astype(jnp.float32)

    over(count, away)
    over(count, home)


def project_body(gated_ref, weight_ref, token_ref, cot_ref, gain_ref, middle_ref, full_ref, up_ref, send, recv, held, sends, arrivals, far, near, landed, up_sems):
    me = lax.axis_index("tensor")
    other = 1 - me
    greet(other)
    half = token_ref.shape[0]
    up_far = pltpu.make_async_remote_copy(
        src_ref=cot_ref, dst_ref=up_ref.at[span(me, half)], send_sem=up_sems.at[0], recv_sem=up_sems.at[1],
        device_id={"tensor": other}, device_id_type=MESH,
    )
    up_near = pltpu.make_async_copy(cot_ref, up_ref.at[span(me, half)], up_sems.at[2])
    up_near.start()

    def product(rows, place):
        return jnp.dot(gated_ref[rows, :], weight_ref[:, span(place, tile)], preferred_element_type=jnp.float32)

    exchange_products(product, send, recv, middle_ref, sends, arrivals, me, other)
    up_far.start()
    count = half // strip
    copies = lambda place: strip_copies(held, full_ref, me, far, near, landed, place, me, other)

    def step(place):
        rows = span(place, strip)
        middle = token_ref[rows, :].astype(jnp.float32) + middle_ref[rows, :]
        middle_ref[rows, :] = middle
        held[rows, :] = (middle * scale_of(middle) * gain_ref[...]).astype(low)
        for copy in copies(place):
            copy.start()

    over(count, step)

    def finish(place):
        for copy in copies(place):
            copy.wait()

    over(count, finish)
    up_near.wait()
    up_far.wait()


def result_body(hidden_ref, weight_ref, middle_ref, result_ref, send, recv, total, sends, arrivals):
    me = lax.axis_index("tensor")
    other = 1 - me
    greet(other)

    def product(rows, place):
        return jnp.dot(hidden_ref[rows, :], weight_ref[:, span(place, tile)], preferred_element_type=jnp.float32)

    exchange_products(product, send, recv, total, sends, arrivals, me, other)

    def step(place):
        rows = span(place, strip)
        result_ref[rows, :] = (total[rows, :] + middle_ref[rows, :]).astype(low)

    over(total.shape[0] // strip, step)


def nt(former, latter):
    return lax.dot_general(former, latter, (((1,), (1,)), ((), ())), preferred_element_type=jnp.float32)


def back_body(gate_ref, up_ref, gate_weight_ref, up_weight_ref, middle_ref, cot_ref, gain_ref, out_ref, full_ref, part_ref, send, recv, total, held, sends, arrivals, far, near, landed):
    me = lax.axis_index("tensor")
    other = 1 - me
    greet(other)

    def product(rows, place):
        columns = span(place, tile)
        return nt(gate_ref[rows, :], gate_weight_ref[columns, :]) + nt(up_ref[rows, :], up_weight_ref[columns, :])

    exchange_products(product, send, recv, total, sends, arrivals, me, other)
    part_ref[...] = jnp.zeros_like(part_ref)
    count = total.shape[0] // strip
    copies = lambda place: strip_copies(held, full_ref, me, far, near, landed, place, me, other)

    def step(place):
        rows = span(place, strip)
        middle = middle_ref[rows, :]
        scale = scale_of(middle)
        normed = middle * scale
        upstream = total[rows, :]
        weighted = upstream * gain_ref[...]
        push = scale * (weighted - normed * jnp.mean(weighted * normed, axis=1, keepdims=True))
        grad = cot_ref[rows, :].astype(jnp.float32) + push
        out_ref[rows, :] = grad
        held[rows, :] = grad.astype(low)
        for copy in copies(place):
            copy.start()
        part_ref[...] += jnp.sum((upstream * normed).reshape(strip // 8, 8, -1), axis=0)

    over(count, step)

    def finish(place):
        for copy in copies(place):
            copy.wait()

    over(count, finish)


def first_body(query_ref, key_ref, value_ref, gate_ref, forget_ref, wq_ref, wk_ref, wv_ref, wg_ref, wf_ref, grad_ref, token_ref, gain_ref, out_ref, part_ref, send, recv, total, sends, arrivals):
    me = lax.axis_index("tensor")
    other = 1 - me
    greet(other)

    def product(rows, place):
        columns = span(place, tile)
        value = nt(query_ref[rows, :], wq_ref[columns, :]) + nt(key_ref[rows, :], wk_ref[columns, :])
        value = value + nt(value_ref[rows, :], wv_ref[columns, :]) + nt(gate_ref[rows, :], wg_ref[columns, :])
        return value + lax.dot_general(
            forget_ref[:, rows], wf_ref[:, columns], (((0,), (0,)), ((), ())), preferred_element_type=jnp.float32
        )

    exchange_products(product, send, recv, total, sends, arrivals, me, other)
    part_ref[...] = jnp.zeros_like(part_ref)

    def step(place):
        rows = span(place, strip)
        values = token_ref[rows, :].astype(jnp.float32)
        scale = scale_of(values)
        normed = values * scale
        upstream = total[rows, :]
        weighted = upstream * gain_ref[...]
        push = scale * (weighted - normed * jnp.mean(weighted * normed, axis=1, keepdims=True))
        out_ref[rows, :] = grad_ref[rows, :] + push
        part_ref[...] += jnp.sum((upstream * normed).reshape(strip // 8, 8, -1), axis=0)

    over(total.shape[0] // strip, step)


def all_sum_body(bits, part_ref, out_ref, slots, sends, arrivals):
    out_ref[...] = part_ref[...]
    places = {}
    for axis in ("dp", "tensor"):
        places[axis] = lax.axis_index(axis)
    partners = []
    for axis, bit in bits:
        here = places[axis]
        flip = here + (1 << bit) - 2 * (1 << bit) * (here // (1 << bit) % 2)
        partners.append({axis: flip})
    barrier = pltpu.get_barrier_semaphore()
    for partner in partners:
        pl.semaphore_signal(barrier, inc=1, device_id=partner, device_id_type=MESH)
    pl.semaphore_wait(barrier, len(partners))
    for place, partner in enumerate(partners):
        copy = pltpu.make_async_remote_copy(
            src_ref=slots.at[2 * place], dst_ref=slots.at[2 * place + 1], send_sem=sends.at[place],
            recv_sem=arrivals.at[place], device_id=partner, device_id_type=MESH,
        )
        slots[2 * place] = out_ref[...]
        copy.start()
        copy.wait()
        out_ref[...] += slots[2 * place + 1]


vmem = pl.BlockSpec(memory_space=pltpu.VMEM)
anywhere = pl.BlockSpec(memory_space=pl.ANY)
dma = pltpu.SemaphoreType.DMA


def comm_params(identity):
    return pltpu.CompilerParams(collective_id=identity, has_side_effects=True, vmem_limit_bytes=60 * 2**20)


def norm_gather(tokens, gain):
    half, width = tokens.shape
    count = half // strip
    return pl.pallas_call(
        gather_body,
        out_shape=jax.ShapeDtypeStruct((2 * half, width), low),
        in_specs=[vmem, vmem],
        out_specs=anywhere,
        scratch_shapes=[pltpu.VMEM((half, width), low), dma((count,)), dma((count,)), dma((count,))],
        compiler_params=comm_params(0),
        cost_estimate=pl.CostEstimate(flops=8 * half * width, bytes_accessed=12 * half * width, transcendentals=half),
        name="norm_gather",
    )(tokens, gain.reshape(1, width))


def exchange_scratch(half, width):
    count = width // tile
    return [pltpu.VMEM((count, half, tile), low), pltpu.VMEM((count, half, tile), low)], [dma((count,)), dma((count,))]


def project(gated, weight, tokens, cotangent, gain):
    half, width = tokens.shape
    count = half // strip
    buffers, sems = exchange_scratch(half, width)
    return pl.pallas_call(
        project_body,
        out_shape=[
            jax.ShapeDtypeStruct((half, width), jnp.float32),
            jax.ShapeDtypeStruct((2 * half, width), low),
            jax.ShapeDtypeStruct((2 * half, width), low),
        ],
        in_specs=[vmem] * 5,
        out_specs=[vmem, anywhere, anywhere],
        scratch_shapes=buffers + [pltpu.VMEM((half, width), low)] + sems + [dma((count,)), dma((count,)), dma((count,)), dma((3,))],
        compiler_params=comm_params(1),
        cost_estimate=pl.CostEstimate(flops=4 * half * width * weight.shape[0], bytes_accessed=24 * half * width, transcendentals=half),
        name="project",
    )(gated, weight, tokens, cotangent, gain.reshape(1, width))


def result_rows(hidden, weight, middle):
    half, width = middle.shape
    buffers, sems = exchange_scratch(half, width)
    return pl.pallas_call(
        result_body,
        out_shape=jax.ShapeDtypeStruct((half, width), low),
        in_specs=[vmem] * 3,
        out_specs=vmem,
        scratch_shapes=buffers + [pltpu.VMEM((half, width), jnp.float32)] + sems,
        compiler_params=comm_params(2),
        cost_estimate=pl.CostEstimate(flops=4 * half * width * weight.shape[0], bytes_accessed=30 * half * width, transcendentals=0),
        name="result_rows",
    )(hidden, weight, middle)


def middle_back(gate_grad, up_grad, gate_weight, up_weight, middle, cotangent, gain):
    half, width = middle.shape
    count = half // strip
    buffers, sems = exchange_scratch(half, width)
    return pl.pallas_call(
        back_body,
        out_shape=[
            jax.ShapeDtypeStruct((half, width), jnp.float32),
            jax.ShapeDtypeStruct((2 * half, width), low),
            jax.ShapeDtypeStruct((8, width), jnp.float32),
        ],
        in_specs=[vmem] * 7,
        out_specs=[vmem, anywhere, vmem],
        scratch_shapes=buffers
        + [pltpu.VMEM((half, width), jnp.float32), pltpu.VMEM((half, width), low)]
        + sems
        + [dma((count,)), dma((count,)), dma((count,))],
        compiler_params=comm_params(3),
        cost_estimate=pl.CostEstimate(flops=8 * half * width * gate_weight.shape[1], bytes_accessed=50 * half * width, transcendentals=half),
        name="middle_back",
    )(gate_grad, up_grad, gate_weight, up_weight, middle, cotangent, gain.reshape(1, width))


def first_back(query_grad, key_grad, value_grad, outgate_grad, forget_grad, weights, forget_t, middle_grad, tokens, gain):
    half, width = tokens.shape
    buffers, sems = exchange_scratch(half, width)
    return pl.pallas_call(
        first_body,
        out_shape=[
            jax.ShapeDtypeStruct((half, width), jnp.float32),
            jax.ShapeDtypeStruct((8, width), jnp.float32),
        ],
        in_specs=[vmem] * 13,
        out_specs=[vmem, vmem],
        scratch_shapes=buffers + [pltpu.VMEM((half, width), jnp.float32)] + sems,
        compiler_params=comm_params(4),
        cost_estimate=pl.CostEstimate(flops=16 * half * width * query_grad.shape[1], bytes_accessed=40 * half * width, transcendentals=half),
        name="first_back",
    )(query_grad, key_grad, value_grad, outgate_grad, forget_grad, *weights, forget_t, middle_grad, tokens, gain.reshape(1, width))


def all_sum(part):
    bits = [("tensor", bit) for bit in range(lax.axis_size("tensor").bit_length() - 1)]
    bits += [("dp", bit) for bit in range(lax.axis_size("dp").bit_length() - 1)]
    return pl.pallas_call(
        partial(all_sum_body, bits),
        out_shape=jax.ShapeDtypeStruct(part.shape, part.dtype),
        in_specs=[vmem],
        out_specs=vmem,
        scratch_shapes=[pltpu.VMEM((2 * len(bits),) + part.shape, part.dtype), dma((len(bits),)), dma((len(bits),))],
        compiler_params=comm_params(5),
        name="all_sum",
    )(part)


def local(
    tokens,
    segment_ids,
    first_gain,
    query_weight,
    key_weight,
    value_weight,
    outgate_weight,
    forget_weight,
    forget_bias,
    output_weight,
    second_gain,
    gate_weight,
    up_weight,
    down_weight,
    cotangent,
):
    local_heads = forget_weight.shape[1]
    head_dim = query_weight.shape[1] // local_heads
    paired = lax.axis_size("tensor") == 2
    segment = segment_ids[0]
    gather = partial(lax.all_gather, axis_name="tensor", axis=0, tiled=True)
    scatter = partial(lax.psum_scatter, axis_name="tensor", scatter_dimension=0, tiled=True)

    if paired:
        first_all = norm_gather(tokens, first_gain)
    else:
        inputs = tokens.astype(jnp.float32)
        scale_one = norm_scale(inputs)
        normed_one = inputs * scale_one
        first_all = gather((normed_one * first_gain).astype(low))
    query_rows = matmul(first_all, query_weight).astype(low)
    key_rows = matmul(first_all, key_weight).astype(low)
    value_rows = matmul(first_all, value_weight).astype(low)
    outgate = jax.nn.sigmoid(matmul(first_all, outgate_weight))
    logit_t = lax.dot_general(
        forget_weight, first_all, (((0,), (1,)), ((), ())), preferred_element_type=jnp.float32
    ) + forget_bias[:, None]
    mixed_out, gated_out, peaks = attend_forward(
        query_rows, key_rows, value_rows, outgate, logit_t, segment, head_dim
    )
    if paired:
        middle, second_all, upstream = project(gated_out, output_weight, tokens, cotangent, second_gain)
    else:
        middle = inputs + scatter(matmul(gated_out, output_weight))
        scale_two = norm_scale(middle)
        normed_two = middle * scale_two
        second_all = gather((normed_two * second_gain).astype(low))
        upstream = gather(cotangent)
    gate_pre = matmul(second_all, gate_weight)
    up_pre = matmul(second_all, up_weight)
    sigmoid_gate = jax.nn.sigmoid(gate_pre)
    swish_out = gate_pre * sigmoid_gate
    hidden = (swish_out * up_pre).astype(low)
    along, across, deep = (), ((0, 1),), ((0, 2),)
    half = hidden.shape[1] // 2
    hidden_grad = against(upstream, down_weight)
    gate_grad = (
        hidden_grad * up_pre * sigmoid_gate * (1.0 + gate_pre * (1.0 - sigmoid_gate))
    ).astype(low)
    up_grad = (hidden_grad * swish_out).astype(low)
    hidden, gate_grad, up_grad = lax.optimization_barrier((hidden, gate_grad, up_grad))
    down = [
        Flow(inner_rows(upstream, hidden[:, :half]).astype(low), along),
        Flow(inner_rows(upstream, hidden[:, half:]).astype(low), across),
    ]
    gate_grad, up_grad = tie((gate_grad, up_grad), start=down)
    gated = [
        Flow(inner_rows(second_all, gate_grad).astype(low), along),
        Flow(inner_rows(second_all, up_grad).astype(low), across),
    ]
    gate_grad, up_grad = tie((gate_grad, up_grad), start=gated, end=down)
    gate_grad, up_grad = tie((gate_grad, up_grad), start=down)
    if paired:
        middle_grad, middle_all, gain_two_part = middle_back(
            gate_grad, up_grad, gate_weight, up_weight, middle, cotangent, second_gain
        )
    else:
        second_grad = scatter(against(gate_grad, gate_weight) + against(up_grad, up_weight))
        middle_grad = cotangent.astype(jnp.float32) + norm_back(
            second_grad, normed_two, scale_two, second_gain
        )
        gain_two_part = jnp.sum(second_grad * normed_two, axis=0, keepdims=True)
        middle_all = gather(middle_grad.astype(low))
    middle_all, outgate = tie((middle_all, outgate), end=down)
    down = [merged(down)]
    middle_all, outgate = tie((middle_all, outgate), start=down)
    gated_grad = against(middle_all, output_weight)
    mixed_grad = (gated_grad * outgate).astype(low)
    outgate_grad = (gated_grad * mixed_out * outgate * (1.0 - outgate)).astype(low)
    width = query_weight.shape[1]
    shared = Flow(
        [inner_rows(middle_all, gated_out).astype(low), inner_rows(first_all, outgate_grad).astype(low)],
        deep,
    )
    mixed_grad = tie(mixed_grad, start=[shared])
    query_grad, key_grad, value_grad, forget_rows = attend_backward(
        query_rows, key_rows, value_rows, mixed_grad, peaks, logit_t, segment, head_dim
    )
    query_grad, key_grad, value_grad, forget_rows = tie(
        (query_grad, key_grad, value_grad, forget_rows), end=down + gated
    )
    query_grad, key_grad, value_grad, forget_rows = tie(
        (query_grad, key_grad, value_grad, forget_rows), start=down + gated
    )
    forget_grad = forget_rows[:local_heads]
    spare = -(query_weight.shape[1] + local_heads) % 128
    grad_forget = lax.dot_general(
        first_all, jnp.pad(forget_grad, ((0, spare), (0, 0))), (((0,), (1,)), ((), ())),
        preferred_element_type=jnp.float32,
    )
    inward = [
        Flow(
            [inner_rows(first_all, query_grad).astype(low), grad_forget.astype(low)],
            along,
        ),
        Flow(inner_rows(first_all, key_grad).astype(low), across),
        Flow(inner_rows(first_all, value_grad).astype(low), deep),
    ]
    query_grad, hidden = tie((query_grad, hidden), start=inward)
    if paired:
        result = result_rows(hidden, down_weight, middle)
    else:
        rows = scatter(matmul(hidden, down_weight).astype(low)).astype(jnp.float32)
        result = (middle + rows).astype(low)
    result, query_grad = tie((result, query_grad), end=gated + [shared])
    gated = [merged(gated)]
    query_grad = tie(query_grad, start=gated + [shared])
    bias_part = jnp.sum(forget_grad.astype(jnp.float32), axis=1)
    forget_t = forget_weight.T
    if paired:
        forget_t = jnp.pad(forget_t, ((0, forget_rows.shape[0] - local_heads), (0, 0)))
        weights = (query_weight, key_weight, value_weight, outgate_weight)
        tokens_grad, gain_one_part = first_back(
            query_grad, key_grad, value_grad, outgate_grad, forget_rows, weights, forget_t,
            middle_grad, tokens, first_gain,
        )
    else:
        total = against(query_grad, query_weight)
        total = total + against(key_grad, key_weight)
        total = total + against(value_grad, value_weight)
        total = total + against(outgate_grad, outgate_weight)
        total = total + inner_rows(forget_grad, forget_t)
        first_grad = scatter(total.astype(low)).astype(jnp.float32)
        tokens_grad = middle_grad + norm_back(first_grad, normed_one, scale_one, first_gain)
        gain_one_part = jnp.sum(first_grad * normed_one, axis=0, keepdims=True)
    all_heads = local_heads * lax.axis_size("tensor")
    placed = lax.dynamic_update_slice(
        jnp.zeros((1, tokens.shape[1]), jnp.float32),
        bias_part[None],
        (0, lax.axis_index("tensor") * local_heads),
    )
    shares = jnp.concatenate(
        [
            jnp.sum(gain_one_part, axis=0, keepdims=True),
            jnp.sum(gain_two_part, axis=0, keepdims=True),
            placed,
            jnp.zeros((5, tokens.shape[1]), jnp.float32),
        ]
    )
    live = down + gated + [shared] + inward
    tokens_grad, shares = tie((tokens_grad, shares), end=live)
    while True:
        flying = [flow for flow in live if not flow.done()]
        last = all(flow.stage == flow.bits - 1 for flow in flying)
        shares = tie(shares, start=flying)
        if last:
            shares = all_sum(shares)
        shares = tie(shares, end=flying)
        if inward[0].stage == 2:
            inward[:2] = [merged(inward[:2])]
            live = [flow for flow in live if flow not in flying] + [shared] + gated + down + inward
            live = list(dict.fromkeys(live))
        if last:
            break
    sums = shares
    inner = inward[0].whole
    shared_part = shared.whole
    after = inner.shape[1] - width
    return (
        result,
        tokens_grad,
        sums[0],
        inner[:, :width],
        inner[:, after:],
        inward[1].whole,
        shared_part[:, width:],
        inner[:, width : width + local_heads],
        sums[2, :all_heads],
        shared_part[:, :width].T,
        sums[1],
        gated[0].whole[:, : gate_weight.shape[1]],
        gated[0].whole[:, gate_weight.shape[1] :],
        down[0].whole.T,
    )


def solution(mesh):
    in_specs = (
        P(("dp", "tensor"), None),
        P("dp", None),
        P(),
        P(None, "tensor"),
        P(None, "tensor"),
        P(None, "tensor"),
        P(None, "tensor"),
        P(None, "tensor"),
        P("tensor"),
        P("tensor", None),
        P(),
        P(None, "tensor"),
        P(None, "tensor"),
        P("tensor", None),
        P(("dp", "tensor"), None),
    )
    out_specs = (
        P(("dp", "tensor"), None),
        P(("dp", "tensor"), None),
        P(),
        P("dp", "tensor"),
        P("dp", "tensor"),
        P("dp", "tensor"),
        P("dp", "tensor"),
        P("dp", "tensor"),
        P(),
        P("tensor", "dp"),
        P(),
        P("dp", "tensor"),
        P("dp", "tensor"),
        P("tensor", "dp"),
    )
    return jax.shard_map(local, mesh=mesh, in_specs=in_specs, out_specs=out_specs, check_vma=False)
```

```python
from functools import partial

import jax
import jax.numpy as jnp
from jax import lax
from jax.experimental import pallas as pl
from jax.experimental.pallas import tpu as pltpu
from jax.sharding import PartitionSpec as P

epsilon = 1e-06
masked_value = -1e30


def matmul(former, latter):
    return jnp.dot(former, latter, preferred_element_type=jnp.float32)


def inner_rows(former, latter):
    return lax.dot_general(
        former, latter, (((0,), (0,)), ((), ())), preferred_element_type=jnp.float32
    )


def against(former, latter):
    return lax.dot_general(
        former, latter, (((1,), (1,)), ((), ())), preferred_element_type=jnp.float32
    )


def norm_scale(matrix):
    return lax.rsqrt(jnp.mean(matrix * matrix, axis=1, keepdims=True) + epsilon)


def norm_back(upstream, normed, scaling, gain_vec):
    weighted = upstream * gain_vec
    return scaling * (weighted - normed * jnp.mean(weighted * normed, axis=1, keepdims=True))


class Flow:
    def __init__(self, gradient, swap):
        self.count = lax.axis_size("dp")
        self.bits = self.count.bit_length() - 1
        self.order = list(range(self.bits))
        for front, back in swap:
            self.order[front], self.order[back] = self.order[back], self.order[front]
        self.live = list(range(self.bits - 1, -1, -1))
        gradients = gradient if isinstance(gradient, list) else [gradient]
        self.wholes = [
            one.reshape((2,) * self.bits + (one.shape[0] // self.count, one.shape[1]))
            for one in gradients
        ]
        self.stage = 0
        self.cut()

    def cut(self):
        bit = self.order[self.stage]
        axis = self.live.index(bit)
        self.live.pop(axis)
        mine = (lax.axis_index("dp") >> bit) & 1
        pick = lambda side: jnp.concatenate(
            [lax.dynamic_index_in_dim(one, side, axis, keepdims=False) for one in self.wholes], axis=-1
        )
        self.sent, self.kept = pick(1 - mine), pick(mine)

    def fly(self):
        bit = self.order[self.stage]
        pairs = [(place, place ^ (1 << bit)) for place in range(self.count)]
        self.got = lax.ppermute(self.sent, "dp", pairs)

    def land(self):
        total = self.kept.astype(jnp.float32) + self.got.astype(jnp.float32)
        self.stage += 1
        if self.stage == self.bits:
            self.whole = total
            return
        self.wholes = [total.astype(jnp.bfloat16)]
        self.cut()

    def done(self):
        return self.stage == self.bits


def merged(flows):
    front = flows[0]
    front.sent = jnp.concatenate([flow.sent for flow in flows], axis=-1)
    front.kept = jnp.concatenate([flow.kept for flow in flows], axis=-1)
    return front


def tie(values, start=(), end=()):
    values, sent, got = lax.optimization_barrier(
        (values, tuple(flow.sent for flow in start), tuple(flow.got for flow in end))
    )
    for flow, one in zip(start, sent):
        flow.sent = one
        flow.fly()
    for flow, one in zip(end, got):
        flow.got = one
        flow.land()
    return values


block_rows = 256
longest_doc = 512
low = jnp.bfloat16
log2e = 1.4426950408889634


def windows(length):
    reach = -(-(longest_doc - 1) // block_rows)
    spans = []
    place = 0
    for one in range(length // block_rows):
        start = max(0, one - reach) * block_rows
        width = (one + 1) * block_rows - start
        spans.append((one * block_rows, start, width, place))
        place += width
    return spans, place


def lane_of(shape):
    return lax.broadcasted_iota(jnp.int32, shape, len(shape) - 1)


def running(rows, back):
    length = rows.shape[1]
    lanes = lane_of(rows.shape)
    step = 1
    while step < length:
        if back:
            moved = jnp.where(lanes < length - step, pltpu.roll(rows, length - step, 1), 0.0)
        else:
            moved = jnp.where(lanes >= step, pltpu.roll(rows, step, 1), 0.0)
        rows = rows + moved
        step *= 2
    return rows


def log_sigmoid(value):
    return jnp.minimum(value, 0.0) - jnp.log1p(jnp.exp(-jnp.abs(value)))


def fill_bias(seg_col, seg_row, bias, spans):
    for first, start, width, place in spans:
        rows = first + lax.broadcasted_iota(jnp.int32, (block_rows, width), 0)
        cols = start + lax.broadcasted_iota(jnp.int32, (block_rows, width), 1)
        same = seg_col[first : first + block_rows, :] == seg_row[:, start : start + width]
        bias[:, place : place + width] = jnp.where((cols <= rows) & same, 0.0, masked_value)


def head_parts(block, head_dim, head, mark):
    lanes = lane_of(block.shape)
    kept = jnp.where(lanes // head_dim == head, block, jnp.zeros_like(block))
    if mark is None:
        return kept
    return jnp.where(lanes == mark, jnp.ones_like(block), kept)


def forward_body(q_ref, k_ref, v_ref, gate_ref, logit_ref, col_ref, row_ref, mixed_ref, gated_ref, peak_ref, bias, fall, *, head_dim, spans, heads):
    pair = pl.program_id(0)

    @pl.when(pair == 0)
    def _():
        fill_bias(col_ref[...], row_ref[...], bias, spans)
        fall[...] = running(log_sigmoid(logit_ref[...]), False) * log2e

    lanes = lane_of((block_rows, q_ref.shape[1]))
    falls = [fall[pl.ds(pair * heads + head, 1), :] for head in range(heads)]
    for first, start, width, place in spans:
        query = q_ref[first : first + block_rows, :]
        key = k_ref[start : start + width, :]
        value = v_ref[start : start + width, :]
        mixed = None
        peaks = None
        for head in range(heads):
            line = falls[head]
            shift = line[:, first : first + 1] - line[:, start : start + width]
            scores = lax.dot_general(
                head_parts(query, head_dim, head, None), key, (((1,), (1,)), ((), ())),
                preferred_element_type=jnp.float32,
            )
            scores = scores * (head_dim**-0.5 * log2e) + shift + bias[:, place : place + width]
            top = jnp.max(scores, axis=1, keepdims=True)
            weight = jnp.exp2(scores - top)
            total = jnp.sum(weight, axis=1, keepdims=True)
            weight = (weight * (1.0 / total)).astype(low)
            part = jnp.dot(weight, head_parts(value, head_dim, head, None), preferred_element_type=jnp.float32)
            peak = jnp.broadcast_to(top + jnp.log2(total), lanes.shape)
            mixed = part if mixed is None else mixed + part
            peaks = peak if peaks is None else jnp.where(lanes // head_dim == head, peak, peaks)
        rows = slice(first, first + block_rows)
        mixed_ref[rows, :] = mixed
        peak_ref[rows, :] = peaks
        gated_ref[rows, :] = (mixed * gate_ref[rows, :]).astype(low)


def attention_sizes(width, head_dim):
    wide = 128 if width % 128 == 0 and 128 % head_dim == 0 else width
    return wide, wide // head_dim


def attend_forward(query, key, value, outgate, logit_t, segment, head_dim):
    length, width = query.shape
    wide, heads = attention_sizes(width, head_dim)
    spans, total = windows(length)
    whole = pl.BlockSpec(memory_space=pltpu.VMEM)
    part = pl.BlockSpec((length, wide), lambda i: (0, i))
    rows = -(-logit_t.shape[0] // 8) * 8
    area = sum(span[2] for span in spans) * block_rows
    return pl.pallas_call(
        partial(forward_body, head_dim=head_dim, spans=spans, heads=heads),
        grid=(width // wide,),
        in_specs=[part, part, part, part, whole, whole, whole],
        out_specs=[part, part, part],
        out_shape=[
            jax.ShapeDtypeStruct((length, width), jnp.float32),
            jax.ShapeDtypeStruct((length, width), low),
            jax.ShapeDtypeStruct((length, width), jnp.float32),
        ],
        scratch_shapes=[
            pltpu.VMEM((block_rows, total), jnp.float32),
            pltpu.VMEM((rows, length), jnp.float32),
        ],
        compiler_params=pltpu.CompilerParams(vmem_limit_bytes=50 * 2**20),
        cost_estimate=pl.CostEstimate(
            flops=16 * area * width, bytes_accessed=20 * length * width, transcendentals=area * width // head_dim
        ),
        name="attend_forward",
    )(query, key, value, outgate, jnp.pad(logit_t, ((0, rows - logit_t.shape[0]), (0, 0))), segment.reshape(length, 1), segment.reshape(1, length))


def backward_body(q_ref, k_ref, v_ref, grad_ref, peak_ref, logit_ref, col_ref, row_ref, dq_ref, dk_ref, dv_ref, forget_ref, bias, fall, key_sum, value_sum, slope, *, head_dim, spans, heads):
    pair = pl.program_id(0)
    wide = q_ref.shape[1]

    @pl.when(pair == 0)
    def _():
        fill_bias(col_ref[...], row_ref[...], bias, spans)
        fall[...] = running(log_sigmoid(logit_ref[...]), False) * log2e
        slope[...] = jnp.zeros_like(slope)

    falls = [fall[pl.ds(pair * heads + head, 1), :] for head in range(heads)]
    scaling = head_dim**-0.5
    value_sum[...] = jnp.zeros_like(value_sum)
    key_sum[...] = jnp.zeros_like(key_sum)
    lanes = lane_of((block_rows, wide))
    slots = lane_of((block_rows, slope.shape[1]))
    marks = [((head + 1) * head_dim) % wide for head in range(heads)]
    for first, start, width, place in spans:
        rows = slice(first, first + block_rows)
        query = q_ref[rows, :]
        key = k_ref[start : start + width, :]
        value = v_ref[start : start + width, :]
        grad = grad_ref[rows, :]
        query_grad = None
        for head in range(heads):
            line = falls[head]
            shift = line[:, first : first + 1] - line[:, start : start + width]
            scores = lax.dot_general(
                head_parts(query, head_dim, head, None), key, (((1,), (1,)), ((), ())),
                preferred_element_type=jnp.float32,
            )
            peak = peak_ref[rows, head * head_dim : head * head_dim + 1]
            scores = scores * (scaling * log2e) + shift + bias[:, place : place + width]
            weight = jnp.exp2(scores - peak)
            own_grad = head_parts(grad, head_dim, head, None)
            rise = lax.dot_general(
                own_grad, value, (((1,), (1,)), ((), ())), preferred_element_type=jnp.float32
            )
            delta = jnp.sum(weight * rise, axis=1, keepdims=True)
            change = (weight * (rise - delta)).astype(low)
            weight = weight.astype(low)
            value_sum[start : start + width, :] += lax.dot_general(
                weight, own_grad, (((0,), (0,)), ((), ())), preferred_element_type=jnp.float32
            )
            mark = marks[head]
            from_key = jnp.dot(change, head_parts(key, head_dim, head, mark), preferred_element_type=jnp.float32)
            key_sum[head, start : start + width, :] += lax.dot_general(
                change, head_parts(query, head_dim, head, mark), (((0,), (0,)), ((), ())),
                preferred_element_type=jnp.float32,
            )
            slope[rows, :] += jnp.where(slots == pair * heads + head, from_key[:, mark : mark + 1], 0.0)
            query_grad = from_key if query_grad is None else jnp.where(lanes // head_dim == head, from_key, query_grad)
        dq_ref[rows, :] = (query_grad * scaling).astype(low)
    length = q_ref.shape[0]
    lanes = lane_of((length, wide))
    slots = lane_of(slope.shape)
    total = key_sum[0]
    gone = jnp.where(slots == pair * heads, total[:, marks[0] : marks[0] + 1], 0.0)
    for head in range(1, heads):
        other = key_sum[head]
        gone += jnp.where(slots == pair * heads + head, other[:, marks[head] : marks[head] + 1], 0.0)
        total = jnp.where(lanes // head_dim == head, other, total)
    slope[...] -= gone
    dk_ref[...] = (total * scaling).astype(low)
    dv_ref[...] = value_sum[...].astype(low)

    @pl.when(pair == pl.num_programs(0) - 1)
    def _():
        count = logit_ref.shape[0]
        turned = slope[...].T[:count, :]
        forget_ref[...] = (running(turned, True) * jax.nn.sigmoid(-logit_ref[...])).astype(low)


def attend_backward(query, key, value, mixed_grad, peaks, logit_t, segment, head_dim):
    length, width = query.shape
    wide, heads = attention_sizes(width, head_dim)
    spans, total = windows(length)
    whole = pl.BlockSpec(memory_space=pltpu.VMEM)
    part = pl.BlockSpec((length, wide), lambda i: (0, i))
    rows = -(-logit_t.shape[0] // 8) * 8
    area = sum(span[2] for span in spans) * block_rows
    return pl.pallas_call(
        partial(backward_body, head_dim=head_dim, spans=spans, heads=heads),
        grid=(width // wide,),
        in_specs=[part, part, part, part, part, whole, whole, whole],
        out_specs=[part, part, part, pl.BlockSpec((rows, length), lambda i: (0, 0))],
        out_shape=[jax.ShapeDtypeStruct((length, width), low)] * 3
        + [jax.ShapeDtypeStruct((rows, length), low)],
        scratch_shapes=[
            pltpu.VMEM((block_rows, total), jnp.float32),
            pltpu.VMEM((rows, length), jnp.float32),
            pltpu.VMEM((heads, length, wide), jnp.float32),
            pltpu.VMEM((length, wide), jnp.float32),
            pltpu.VMEM((length, 128), jnp.float32),
        ],
        compiler_params=pltpu.CompilerParams(vmem_limit_bytes=50 * 2**20),
        cost_estimate=pl.CostEstimate(
            flops=40 * area * width, bytes_accessed=20 * length * width, transcendentals=area * width // head_dim
        ),
        name="attend_backward",
    )(query, key, value, mixed_grad, peaks, jnp.pad(logit_t, ((0, rows - logit_t.shape[0]), (0, 0))), segment.reshape(length, 1), segment.reshape(1, length))


MESH = pl.DeviceIdType.MESH
tile = 256
strip = 64


def greet(other):
    barrier = pltpu.get_barrier_semaphore()
    pl.semaphore_signal(barrier, inc=1, device_id={"tensor": other}, device_id_type=MESH)
    pl.semaphore_wait(barrier, 1)


def over(count, body):
    lax.fori_loop(0, count, lambda place, carry: (body(place), carry)[1], 0)


def span(place, size):
    return pl.ds(pl.multiple_of(place * size, size), size)


def to_other(source, target, sends, arrivals, place, other):
    return pltpu.make_async_remote_copy(
        src_ref=source,
        dst_ref=target,
        send_sem=sends.at[place],
        recv_sem=arrivals.at[place],
        device_id={"tensor": other},
        device_id_type=MESH,
    )


def scale_of(rows):
    return lax.rsqrt(jnp.mean(rows * rows, axis=1, keepdims=True) + epsilon)


def strip_copies(held, full, own, far, near, arrivals, place, me, other):
    half = held.shape[0]
    rows = span(place, strip)
    into = pl.ds(pl.multiple_of(me * half + place * strip, strip), strip)
    remote = to_other(held.at[rows], full.at[into], far, arrivals, place, other)
    return remote, pltpu.make_async_copy(held.at[rows], full.at[into], near.at[place])


def gather_body(token_ref, gain_ref, full_ref, held, far, near, arrivals):
    me = lax.axis_index("tensor")
    other = 1 - me
    greet(other)
    count = held.shape[0] // strip
    copies = lambda place: strip_copies(held, full_ref, me, far, near, arrivals, place, me, other)

    def step(place):
        rows = span(place, strip)
        values = token_ref[rows, :].astype(jnp.float32)
        held[rows, :] = (values * scale_of(values) * gain_ref[...]).astype(low)
        for copy in copies(place):
            copy.start()

    over(count, step)

    def finish(place):
        for copy in copies(place):
            copy.wait()

    over(count, finish)


def exchange_products(product, send, recv, total, sends, arrivals, me, other):
    half = total.shape[0]
    count = total.shape[1] // tile
    copy = lambda place: to_other(send.at[place], recv.at[place], sends, arrivals, place, other)

    def away(place):
        send[place] = product(span(other, half), place).astype(low)
        copy(place).start()

    def home(place):
        columns = span(place, tile)
        total[:, columns] = product(span(me, half), place)
        copy(place).wait()
        total[:, columns] += recv[place].astype(jnp.float32)

    over(count, away)
    over(count, home)


def project_body(gated_ref, weight_ref, token_ref, cot_ref, gain_ref, middle_ref, full_ref, up_ref, send, recv, held, sends, arrivals, far, near, landed, up_sems):
    me = lax.axis_index("tensor")
    other = 1 - me
    greet(other)
    half = token_ref.shape[0]
    up_far = pltpu.make_async_remote_copy(
        src_ref=cot_ref, dst_ref=up_ref.at[span(me, half)], send_sem=up_sems.at[0], recv_sem=up_sems.at[1],
        device_id={"tensor": other}, device_id_type=MESH,
    )
    up_near = pltpu.make_async_copy(cot_ref, up_ref.at[span(me, half)], up_sems.at[2])
    up_near.start()

    def product(rows, place):
        return jnp.dot(gated_ref[rows, :], weight_ref[:, span(place, tile)], preferred_element_type=jnp.float32)

    exchange_products(product, send, recv, middle_ref, sends, arrivals, me, other)
    up_far.start()
    count = half // strip
    copies = lambda place: strip_copies(held, full_ref, me, far, near, landed, place, me, other)

    def step(place):
        rows = span(place, strip)
        middle = token_ref[rows, :].astype(jnp.float32) + middle_ref[rows, :]
        middle_ref[rows, :] = middle
        held[rows, :] = (middle * scale_of(middle) * gain_ref[...]).astype(low)
        for copy in copies(place):
            copy.start()

    over(count, step)

    def finish(place):
        for copy in copies(place):
            copy.wait()

    over(count, finish)
    up_near.wait()
    up_far.wait()


def result_body(hidden_ref, weight_ref, middle_ref, result_ref, send, recv, total, sends, arrivals):
    me = lax.axis_index("tensor")
    other = 1 - me
    greet(other)

    def product(rows, place):
        return jnp.dot(hidden_ref[rows, :], weight_ref[:, span(place, tile)], preferred_element_type=jnp.float32)

    exchange_products(product, send, recv, total, sends, arrivals, me, other)

    def step(place):
        rows = span(place, strip)
        result_ref[rows, :] = (total[rows, :] + middle_ref[rows, :]).astype(low)

    over(total.shape[0] // strip, step)


def nt(former, latter):
    return lax.dot_general(former, latter, (((1,), (1,)), ((), ())), preferred_element_type=jnp.float32)


def back_body(gate_ref, up_ref, gate_weight_ref, up_weight_ref, middle_ref, cot_ref, gain_ref, out_ref, full_ref, part_ref, send, recv, total, held, sends, arrivals, far, near, landed):
    me = lax.axis_index("tensor")
    other = 1 - me
    greet(other)

    def product(rows, place):
        columns = span(place, tile)
        return nt(gate_ref[rows, :], gate_weight_ref[columns, :]) + nt(up_ref[rows, :], up_weight_ref[columns, :])

    exchange_products(product, send, recv, total, sends, arrivals, me, other)
    part_ref[...] = jnp.zeros_like(part_ref)
    count = total.shape[0] // strip
    copies = lambda place: strip_copies(held, full_ref, me, far, near, landed, place, me, other)

    def step(place):
        rows = span(place, strip)
        middle = middle_ref[rows, :]
        scale = scale_of(middle)
        normed = middle * scale
        upstream = total[rows, :]
        weighted = upstream * gain_ref[...]
        push = scale * (weighted - normed * jnp.mean(weighted * normed, axis=1, keepdims=True))
        grad = cot_ref[rows, :].astype(jnp.float32) + push
        out_ref[rows, :] = grad
        held[rows, :] = grad.astype(low)
        for copy in copies(place):
            copy.start()
        part_ref[...] += jnp.sum((upstream * normed).reshape(strip // 8, 8, -1), axis=0)

    over(count, step)

    def finish(place):
        for copy in copies(place):
            copy.wait()

    over(count, finish)


def first_body(query_ref, key_ref, value_ref, gate_ref, forget_ref, wq_ref, wk_ref, wv_ref, wg_ref, wf_ref, grad_ref, token_ref, gain_ref, out_ref, part_ref, send, recv, total, sends, arrivals):
    me = lax.axis_index("tensor")
    other = 1 - me
    greet(other)

    def product(rows, place):
        columns = span(place, tile)
        value = nt(query_ref[rows, :], wq_ref[columns, :]) + nt(key_ref[rows, :], wk_ref[columns, :])
        value = value + nt(value_ref[rows, :], wv_ref[columns, :]) + nt(gate_ref[rows, :], wg_ref[columns, :])
        return value + lax.dot_general(
            forget_ref[:, rows], wf_ref[:, columns], (((0,), (0,)), ((), ())), preferred_element_type=jnp.float32
        )

    exchange_products(product, send, recv, total, sends, arrivals, me, other)
    part_ref[...] = jnp.zeros_like(part_ref)

    def step(place):
        rows = span(place, strip)
        values = token_ref[rows, :].astype(jnp.float32)
        scale = scale_of(values)
        normed = values * scale
        upstream = total[rows, :]
        weighted = upstream * gain_ref[...]
        push = scale * (weighted - normed * jnp.mean(weighted * normed, axis=1, keepdims=True))
        out_ref[rows, :] = grad_ref[rows, :] + push
        part_ref[...] += jnp.sum((upstream * normed).reshape(strip // 8, 8, -1), axis=0)

    over(total.shape[0] // strip, step)


def all_sum_body(bits, part_ref, out_ref, slots, sends, arrivals):
    out_ref[...] = part_ref[...]
    places = {}
    for axis in ("dp", "tensor"):
        places[axis] = lax.axis_index(axis)
    partners = []
    for axis, bit in bits:
        here = places[axis]
        flip = here + (1 << bit) - 2 * (1 << bit) * (here // (1 << bit) % 2)
        partners.append({axis: flip})
    barrier = pltpu.get_barrier_semaphore()
    for partner in partners:
        pl.semaphore_signal(barrier, inc=1, device_id=partner, device_id_type=MESH)
    pl.semaphore_wait(barrier, len(partners))
    for place, partner in enumerate(partners):
        copy = pltpu.make_async_remote_copy(
            src_ref=slots.at[2 * place], dst_ref=slots.at[2 * place + 1], send_sem=sends.at[place],
            recv_sem=arrivals.at[place], device_id=partner, device_id_type=MESH,
        )
        slots[2 * place] = out_ref[...]
        copy.start()
        copy.wait()
        out_ref[...] += slots[2 * place + 1]


vmem = pl.BlockSpec(memory_space=pltpu.VMEM)
anywhere = pl.BlockSpec(memory_space=pl.ANY)
dma = pltpu.SemaphoreType.DMA


def comm_params(identity):
    return pltpu.CompilerParams(collective_id=identity, has_side_effects=True, vmem_limit_bytes=60 * 2**20)


def norm_gather(tokens, gain):
    half, width = tokens.shape
    count = half // strip
    return pl.pallas_call(
        gather_body,
        out_shape=jax.ShapeDtypeStruct((2 * half, width), low),
        in_specs=[vmem, vmem],
        out_specs=anywhere,
        scratch_shapes=[pltpu.VMEM((half, width), low), dma((count,)), dma((count,)), dma((count,))],
        compiler_params=comm_params(0),
        cost_estimate=pl.CostEstimate(flops=8 * half * width, bytes_accessed=12 * half * width, transcendentals=half),
        name="norm_gather",
    )(tokens, gain.reshape(1, width))


def exchange_scratch(half, width):
    count = width // tile
    return [pltpu.VMEM((count, half, tile), low), pltpu.VMEM((count, half, tile), low)], [dma((count,)), dma((count,))]


def project(gated, weight, tokens, cotangent, gain):
    half, width = tokens.shape
    count = half // strip
    buffers, sems = exchange_scratch(half, width)
    return pl.pallas_call(
        project_body,
        out_shape=[
            jax.ShapeDtypeStruct((half, width), jnp.float32),
            jax.ShapeDtypeStruct((2 * half, width), low),
            jax.ShapeDtypeStruct((2 * half, width), low),
        ],
        in_specs=[vmem] * 5,
        out_specs=[vmem, anywhere, anywhere],
        scratch_shapes=buffers + [pltpu.VMEM((half, width), low)] + sems + [dma((count,)), dma((count,)), dma((count,)), dma((3,))],
        compiler_params=comm_params(1),
        cost_estimate=pl.CostEstimate(flops=4 * half * width * weight.shape[0], bytes_accessed=24 * half * width, transcendentals=half),
        name="project",
    )(gated, weight, tokens, cotangent, gain.reshape(1, width))


def result_rows(hidden, weight, middle):
    half, width = middle.shape
    buffers, sems = exchange_scratch(half, width)
    return pl.pallas_call(
        result_body,
        out_shape=jax.ShapeDtypeStruct((half, width), low),
        in_specs=[vmem] * 3,
        out_specs=vmem,
        scratch_shapes=buffers + [pltpu.VMEM((half, width), jnp.float32)] + sems,
        compiler_params=comm_params(2),
        cost_estimate=pl.CostEstimate(flops=4 * half * width * weight.shape[0], bytes_accessed=30 * half * width, transcendentals=0),
        name="result_rows",
    )(hidden, weight, middle)


def middle_back(gate_grad, up_grad, gate_weight, up_weight, middle, cotangent, gain):
    half, width = middle.shape
    count = half // strip
    buffers, sems = exchange_scratch(half, width)
    return pl.pallas_call(
        back_body,
        out_shape=[
            jax.ShapeDtypeStruct((half, width), jnp.float32),
            jax.ShapeDtypeStruct((2 * half, width), low),
            jax.ShapeDtypeStruct((8, width), jnp.float32),
        ],
        in_specs=[vmem] * 7,
        out_specs=[vmem, anywhere, vmem],
        scratch_shapes=buffers
        + [pltpu.VMEM((half, width), jnp.float32), pltpu.VMEM((half, width), low)]
        + sems
        + [dma((count,)), dma((count,)), dma((count,))],
        compiler_params=comm_params(3),
        cost_estimate=pl.CostEstimate(flops=8 * half * width * gate_weight.shape[1], bytes_accessed=50 * half * width, transcendentals=half),
        name="middle_back",
    )(gate_grad, up_grad, gate_weight, up_weight, middle, cotangent, gain.reshape(1, width))


def first_back(query_grad, key_grad, value_grad, outgate_grad, forget_grad, weights, forget_t, middle_grad, tokens, gain):
    half, width = tokens.shape
    buffers, sems = exchange_scratch(half, width)
    return pl.pallas_call(
        first_body,
        out_shape=[
            jax.ShapeDtypeStruct((half, width), jnp.float32),
            jax.ShapeDtypeStruct((8, width), jnp.float32),
        ],
        in_specs=[vmem] * 13,
        out_specs=[vmem, vmem],
        scratch_shapes=buffers + [pltpu.VMEM((half, width), jnp.float32)] + sems,
        compiler_params=comm_params(4),
        cost_estimate=pl.CostEstimate(flops=16 * half * width * query_grad.shape[1], bytes_accessed=40 * half * width, transcendentals=half),
        name="first_back",
    )(query_grad, key_grad, value_grad, outgate_grad, forget_grad, *weights, forget_t, middle_grad, tokens, gain.reshape(1, width))


def all_sum(part):
    bits = [("tensor", bit) for bit in range(lax.axis_size("tensor").bit_length() - 1)]
    bits += [("dp", bit) for bit in range(lax.axis_size("dp").bit_length() - 1)]
    return pl.pallas_call(
        partial(all_sum_body, bits),
        out_shape=jax.ShapeDtypeStruct(part.shape, part.dtype),
        in_specs=[vmem],
        out_specs=vmem,
        scratch_shapes=[pltpu.VMEM((2 * len(bits),) + part.shape, part.dtype), dma((len(bits),)), dma((len(bits),))],
        compiler_params=comm_params(5),
        name="all_sum",
    )(part)


def local(
    tokens,
    segment_ids,
    first_gain,
    query_weight,
    key_weight,
    value_weight,
    outgate_weight,
    forget_weight,
    forget_bias,
    output_weight,
    second_gain,
    gate_weight,
    up_weight,
    down_weight,
    cotangent,
):
    local_heads = forget_weight.shape[1]
    head_dim = query_weight.shape[1] // local_heads
    paired = lax.axis_size("tensor") == 2
    segment = segment_ids[0]
    gather = partial(lax.all_gather, axis_name="tensor", axis=0, tiled=True)
    scatter = partial(lax.psum_scatter, axis_name="tensor", scatter_dimension=0, tiled=True)

    if paired:
        first_all = norm_gather(tokens, first_gain)
    else:
        inputs = tokens.astype(jnp.float32)
        scale_one = norm_scale(inputs)
        normed_one = inputs * scale_one
        first_all = gather((normed_one * first_gain).astype(low))
    query_rows = matmul(first_all, query_weight).astype(low)
    key_rows = matmul(first_all, key_weight).astype(low)
    value_rows = matmul(first_all, value_weight).astype(low)
    outgate = jax.nn.sigmoid(matmul(first_all, outgate_weight))
    logit_t = lax.dot_general(
        forget_weight, first_all, (((0,), (1,)), ((), ())), preferred_element_type=jnp.float32
    ) + forget_bias[:, None]
    mixed_out, gated_out, peaks = attend_forward(
        query_rows, key_rows, value_rows, outgate, logit_t, segment, head_dim
    )
    if paired:
        middle, second_all, upstream = project(gated_out, output_weight, tokens, cotangent, second_gain)
    else:
        middle = inputs + scatter(matmul(gated_out, output_weight))
        scale_two = norm_scale(middle)
        normed_two = middle * scale_two
        second_all = gather((normed_two * second_gain).astype(low))
        upstream = gather(cotangent)
    gate_pre = matmul(second_all, gate_weight)
    up_pre = matmul(second_all, up_weight)
    sigmoid_gate = jax.nn.sigmoid(gate_pre)
    swish_out = gate_pre * sigmoid_gate
    hidden = (swish_out * up_pre).astype(low)
    along, across, deep = (), ((0, 1),), ((0, 2),)
    half = hidden.shape[1] // 2
    hidden_grad = against(upstream, down_weight)
    gate_grad = (
        hidden_grad * up_pre * sigmoid_gate * (1.0 + gate_pre * (1.0 - sigmoid_gate))
    ).astype(low)
    up_grad = (hidden_grad * swish_out).astype(low)
    hidden, gate_grad, up_grad = lax.optimization_barrier((hidden, gate_grad, up_grad))
    down = [
        Flow(inner_rows(upstream, hidden[:, :half]).astype(low), along),
        Flow(inner_rows(upstream, hidden[:, half:]).astype(low), across),
    ]
    gate_grad, up_grad = tie((gate_grad, up_grad), start=down)
    gated = [
        Flow(inner_rows(second_all, gate_grad).astype(low), along),
        Flow(inner_rows(second_all, up_grad).astype(low), across),
    ]
    gate_grad, up_grad = tie((gate_grad, up_grad), start=gated, end=down)
    gate_grad, up_grad = tie((gate_grad, up_grad), start=down)
    if paired:
        middle_grad, middle_all, gain_two_part = middle_back(
            gate_grad, up_grad, gate_weight, up_weight, middle, cotangent, second_gain
        )
    else:
        second_grad = scatter(against(gate_grad, gate_weight) + against(up_grad, up_weight))
        middle_grad = cotangent.astype(jnp.float32) + norm_back(
            second_grad, normed_two, scale_two, second_gain
        )
        gain_two_part = jnp.sum(second_grad * normed_two, axis=0, keepdims=True)
        middle_all = gather(middle_grad.astype(low))
    middle_all, outgate = tie((middle_all, outgate), end=down)
    down = [merged(down)]
    middle_all, outgate = tie((middle_all, outgate), start=down)
    gated_grad = against(middle_all, output_weight)
    mixed_grad = (gated_grad * outgate).astype(low)
    outgate_grad = (gated_grad * mixed_out * outgate * (1.0 - outgate)).astype(low)
    width = query_weight.shape[1]
    shared = Flow(
        [inner_rows(middle_all, gated_out).astype(low), inner_rows(first_all, outgate_grad).astype(low)],
        deep,
    )
    mixed_grad = tie(mixed_grad, start=[shared])
    query_grad, key_grad, value_grad, forget_rows = attend_backward(
        query_rows, key_rows, value_rows, mixed_grad, peaks, logit_t, segment, head_dim
    )
    query_grad, key_grad, value_grad, forget_rows = tie(
        (query_grad, key_grad, value_grad, forget_rows), end=down + gated
    )
    query_grad, key_grad, value_grad, forget_rows = tie(
        (query_grad, key_grad, value_grad, forget_rows), start=down + gated
    )
    forget_grad = forget_rows[:local_heads]
    spare = -(query_weight.shape[1] + local_heads) % 128
    grad_forget = lax.dot_general(
        first_all, jnp.pad(forget_grad, ((0, spare), (0, 0))), (((0,), (1,)), ((), ())),
        preferred_element_type=jnp.float32,
    )
    inward = [
        Flow(
            [inner_rows(first_all, query_grad).astype(low), grad_forget.astype(low)],
            along,
        ),
        Flow(inner_rows(first_all, key_grad).astype(low), across),
        Flow(inner_rows(first_all, value_grad).astype(low), deep),
    ]
    query_grad, hidden = tie((query_grad, hidden), start=inward)
    if paired:
        result = result_rows(hidden, down_weight, middle)
    else:
        rows = scatter(matmul(hidden, down_weight).astype(low)).astype(jnp.float32)
        result = (middle + rows).astype(low)
    result, query_grad = tie((result, query_grad), end=gated + [shared])
    gated = [merged(gated)]
    query_grad = tie(query_grad, start=gated + [shared])
    bias_part = jnp.sum(forget_grad.astype(jnp.float32), axis=1)
    forget_t = forget_weight.T
    if paired:
        forget_t = jnp.pad(forget_t, ((0, forget_rows.shape[0] - local_heads), (0, 0)))
        weights = (query_weight, key_weight, value_weight, outgate_weight)
        tokens_grad, gain_one_part = first_back(
            query_grad, key_grad, value_grad, outgate_grad, forget_rows, weights, forget_t,
            middle_grad, tokens, first_gain,
        )
    else:
        total = against(query_grad, query_weight)
        total = total + against(key_grad, key_weight)
        total = total + against(value_grad, value_weight)
        total = total + against(outgate_grad, outgate_weight)
        total = total + inner_rows(forget_grad, forget_t)
        first_grad = scatter(total.astype(low)).astype(jnp.float32)
        tokens_grad = middle_grad + norm_back(first_grad, normed_one, scale_one, first_gain)
        gain_one_part = jnp.sum(first_grad * normed_one, axis=0, keepdims=True)
    all_heads = local_heads * lax.axis_size("tensor")
    placed = lax.dynamic_update_slice(
        jnp.zeros((1, tokens.shape[1]), jnp.float32),
        bias_part[None],
        (0, lax.axis_index("tensor") * local_heads),
    )
    shares = jnp.concatenate(
        [
            jnp.sum(gain_one_part, axis=0, keepdims=True),
            jnp.sum(gain_two_part, axis=0, keepdims=True),
            placed,
            jnp.zeros((5, tokens.shape[1]), jnp.float32),
        ]
    )
    live = down + gated + [shared] + inward
    shares = all_sum(shares)
    tokens_grad, shares = tie((tokens_grad, shares), end=live)
    while True:
        flying = [flow for flow in live if not flow.done()]
        last = all(flow.stage == flow.bits - 1 for flow in flying)
        shares = tie(shares, start=flying)
        shares = tie(shares, end=flying)
        if inward[0].stage == 2:
            inward[:2] = [merged(inward[:2])]
            live = [flow for flow in live if flow not in flying] + [shared] + gated + down + inward
            live = list(dict.fromkeys(live))
        if last:
            break
    sums = shares
    inner = inward[0].whole
    shared_part = shared.whole
    after = inner.shape[1] - width
    return (
        result,
        tokens_grad,
        sums[0],
        inner[:, :width],
        inner[:, after:],
        inward[1].whole,
        shared_part[:, width:],
        inner[:, width : width + local_heads],
        sums[2, :all_heads],
        shared_part[:, :width].T,
        sums[1],
        gated[0].whole[:, : gate_weight.shape[1]],
        gated[0].whole[:, gate_weight.shape[1] :],
        down[0].whole.T,
    )


def solution(mesh):
    in_specs = (
        P(("dp", "tensor"), None),
        P("dp", None),
        P(),
        P(None, "tensor"),
        P(None, "tensor"),
        P(None, "tensor"),
        P(None, "tensor"),
        P(None, "tensor"),
        P("tensor"),
        P("tensor", None),
        P(),
        P(None, "tensor"),
        P(None, "tensor"),
        P("tensor", None),
        P(("dp", "tensor"), None),
    )
    out_specs = (
        P(("dp", "tensor"), None),
        P(("dp", "tensor"), None),
        P(),
        P("dp", "tensor"),
        P("dp", "tensor"),
        P("dp", "tensor"),
        P("dp", "tensor"),
        P("dp", "tensor"),
        P(),
        P("tensor", "dp"),
        P(),
        P("dp", "tensor"),
        P("dp", "tensor"),
        P("tensor", "dp"),
    )
    return jax.shard_map(local, mesh=mesh, in_specs=in_specs, out_specs=out_specs, check_vma=False)
```
